32 devices in a mesh: rows: 16 (over z, y, x), seq: 2 (over core).
Axes of the slice: x: 2, y: 2, z: 4, core: 2. Of those that a mesh axis runs over, the one named last changes fastest.
Arguments:
- tokens: bfloat16 [64, 512, 1024], P('rows', 'seq'), may hold values from -6 to 6
- segments: int32 [64, 512], P('rows'), may hold values from -1 to 9, as said below
- pad_mask: int32 [64, 512], P('rows', 'seq'), may hold values from 0 to 1, as said below
- dest_shard: int32 [64, 10], P('rows'), may hold values from 0 to 1, as said below
- dest_slot: int32 [64, 10], P('rows'), may hold values from 0 to 19, as said below
- ln1_gain: bfloat16 [1024], P(('rows', 'seq')), may hold values from 0.5 to 1.5
- ln1_bias: bfloat16 [1024], P(('rows', 'seq')), may hold values from -1.796875 to 1.796875
- qkv_weight: bfloat16 [1024, 3072], P(('rows', 'seq')), may hold values from -0.1875 to 0.1875
- qv_bias: bfloat16 [2, 1024], P(None, ('rows', 'seq')), may hold values from -3 to 3
- out_weight: bfloat16 [1024, 1024], P(('rows', 'seq')), may hold values from -1.5 to 1.5
- out_bias: bfloat16 [1024], P(('rows', 'seq')), may hold values from -1.796875 to 1.796875
- ln2_gain: bfloat16 [1024], P(('rows', 'seq')), may hold values from 0.5 to 1.5
- ln2_bias: bfloat16 [1024], P(('rows', 'seq')), may hold values from -1.796875 to 1.796875
- fc1_weight: bfloat16 [1024, 4096], P(('rows', 'seq')), may hold values from -0.1875 to 0.1875
- fc1_bias: bfloat16 [4096], P(('rows', 'seq')), may hold values from -3 to 3
- fc2_weight: bfloat16 [4096, 1024], P(('rows', 'seq')), may hold values from -0.09375 to 0.09375
- fc2_bias: bfloat16 [1024], P(('rows', 'seq')), may hold values from -1.796875 to 1.796875
- learn_gain: bfloat16 [1024], replicated, may hold values from 0.5 to 1.5
- learn_bias: bfloat16 [1024], replicated, may hold values from -1.796875 to 1.796875
- maps_weight: bfloat16 [8, 1024], replicated, may hold values from -0.1875 to 0.1875
- maps_bias: bfloat16 [8], replicated, may hold values from -4 to 4
- out_grad: bfloat16 [16, 40, 8, 1024], P('rows', 'seq'), may hold values from -384 to 384
Outputs:
- pooled: bfloat16 [16, 40, 8, 1024], P('rows', 'seq')
- grad_tokens: float32 [64, 512, 1024], P('rows', 'seq')
- grad_ln1_gain: float32 [1024], P(('rows', 'seq'))
- grad_ln1_bias: float32 [1024], P(('rows', 'seq'))
- grad_qkv_weight: float32 [1024, 3072], P(('rows', 'seq'))
- grad_qv_bias: float32 [2, 1024], P(None, ('rows', 'seq'))
- grad_out_weight: float32 [1024, 1024], P(('rows', 'seq'))
- grad_out_bias: float32 [1024], P(('rows', 'seq'))
- grad_ln2_gain: float32 [1024], P(('rows', 'seq'))
- grad_ln2_bias: float32 [1024], P(('rows', 'seq'))
- grad_fc1_weight: float32 [1024, 4096], P(('rows', 'seq'))
- grad_fc1_bias: float32 [4096], P(('rows', 'seq'))
- grad_fc2_weight: float32 [4096, 1024], P(('rows', 'seq'))
- grad_fc2_bias: float32 [1024], P(('rows', 'seq'))
- grad_learn_gain: float32 [1024], replicated
- grad_learn_bias: float32 [1024], replicated
- grad_maps_weight: float32 [8, 1024], replicated
- grad_maps_bias: float32 [8], replicated
The draws below stay inside these ranges and needn't reach their ends.
Inputs may be any that keep to these rules, and one draw needn't show every extreme that they name: `segments`: in each row images are runs of consecutive slots from slot 0, with ids 0, 1, 2, ... in order, each 49, 100 or 196 slots long; the slots after the last image are padding with id -1; in every draw some row holds 10 images. `pad_mask`: 1 exactly on the slots that belong to an image. `dest_shard`: over the 4 rows of one index of rows, records in order (row by row, image id within a row), the k-th existing image (k from 0) goes to seq index (k + c) mod 2 for a c drawn for that index; records without an image hold arbitrary values. `dest_slot`: the k-th existing image of an index of rows takes slot 19 - k // 2, so existing images of one index of rows have distinct (shard, slot) pairs and each device's slots fill from 19 downward; records without an image hold arbitrary slots.
All inputs are finite; a program needn't handle non-finite values.
Results may differ from the reference program's by a relative error of at most 0.0085.
Values may be sent and summed in bfloat16 or wider, within the bound.
No kernel may reach another device: no remote copies, remote signals or barrier semaphores. Data moves between devices by JAX's collectives and lax.ppermute only.
A program may use at most 256 MiB of HBM per device.

```python
import jax
import jax.numpy as jnp
from jax import lax

D = 1024
FF = 4096
HEAD_DIM = 64
NTOK = 8
ROW_LEN = 512
PATCH_S = 49
PATCH_M = 100
PATCH_L = 196
IMG_ROW = 10
ROWS_DEV = 4
ROWS = 64
CAP = 20
N_ROWS = 16
N_SEQ = 2


def packing(key):
    rows_all = ROWS_DEV * N_ROWS
    records = ROWS_DEV * IMG_ROW
    picks = jax.random.randint(jax.random.fold_in(key, 101), (rows_all, IMG_ROW), 0, 10)
    sizes = jnp.where(picks < 5, PATCH_S, jnp.where(picks < 8, PATCH_M, PATCH_L)).astype(jnp.int32)
    full_row = jax.random.randint(jax.random.fold_in(key, 102), (), 0, rows_all)
    row_index = jnp.arange(rows_all, dtype=jnp.int32)[:, None]
    sizes = jnp.where(row_index == full_row, PATCH_S, sizes).astype(jnp.int32)
    ends = jnp.cumsum(sizes, axis=1)
    starts = ends - sizes
    present = ends <= ROW_LEN
    slot_ids = jnp.arange(ROW_LEN, dtype=jnp.int32)[None, :, None]
    inside = present[:, None, :] & (starts[:, None, :] <= slot_ids) & (slot_ids < ends[:, None, :])
    labels = jnp.arange(IMG_ROW, dtype=jnp.int32)[None, None, :] + 1
    segment_ids = (jnp.sum(jnp.where(inside, labels, 0), axis=2) - 1).astype(jnp.int32)
    live = present.reshape(N_ROWS, records).astype(jnp.int32)
    ranks = jnp.cumsum(live, axis=1) - 1
    offsets = jax.random.randint(jax.random.fold_in(key, 103), (N_ROWS, 1), 0, N_SEQ)
    spare_shard = jax.random.randint(jax.random.fold_in(key, 104), (N_ROWS, records), 0, N_SEQ)
    spare_slot = jax.random.randint(jax.random.fold_in(key, 105), (N_ROWS, records), 0, CAP)
    shard_ids = jnp.where(live > 0, (ranks + offsets) % N_SEQ, spare_shard).astype(jnp.int32)
    slot_vals = jnp.where(live > 0, CAP - 1 - ranks // N_SEQ, spare_slot).astype(jnp.int32)
    pad_vals = (segment_ids >= 0).astype(jnp.int32)
    return (segment_ids, pad_vals, shard_ids.reshape(rows_all, IMG_ROW), slot_vals.reshape(rows_all, IMG_ROW))


def draw_segments(key, part):
    return packing(key)[0]


def draw_pad_mask(key, part):
    return packing(key)[1]


def draw_dest_shard(key, part):
    return packing(key)[2]


def draw_dest_slot(key, part):
    return packing(key)[3]


def spiked(values, own_key, source, target, shards_of, factor):
    owner, partner = [(jnp.arange(values.shape[axis_at]) // (values.shape[axis_at] // shards_of)).reshape([-1 if axis == axis_at else 1 for axis in range(values.ndim)]) for axis_at in (source, target)]
    chosen = jax.random.permutation(own_key, shards_of)[partner]
    strong = (owner == chosen) | (owner == (partner + shards_of // 2) % shards_of)
    return jnp.where(strong, factor * values, values)


def levels(stream_key, extent, cuts, smallest, high):
    def one(axis_at, parts):
        heights = jax.random.uniform(jax.random.fold_in(jax.random.fold_in(stream_key, 6), axis_at), (parts,), jnp.float32, smallest / len(cuts), high / len(cuts))
        return jnp.repeat(jnp.exp(heights), extent[axis_at] // parts).reshape((-1,) + (1,) * (len(extent) - axis_at - 1))

    loudness = one(*cuts[0])
    for cut in cuts[1:]:
        loudness = loudness * one(*cut)
    return loudness


def gaussian(own_key, shape, scale, most, split=(), kind=jnp.bfloat16):
    gain = levels(own_key, shape, split, -0.22, 0.18) if split else 1.0
    values = jax.random.normal(own_key, shape, jnp.float32) * scale * gain
    return jnp.minimum(jnp.maximum(values, -most), most).astype(kind)


def gaussian_with(stream_key, dims, scale, reach, split, heavy, kind=jnp.bfloat16):
    array = scale * jax.random.normal(stream_key, dims, jnp.float32)
    if split:
        array = array * levels(stream_key, dims, split, -0.22, 0.18)
    return jnp.clip(spiked(array, jax.random.fold_in(stream_key, 3), *heavy), -reach, reach).astype(kind)


def setup_inputs(seed: int = 0) -> dict:
    splits = jax.random.split(jax.random.key(seed), 23)
    return {
        "tokens": gaussian_with(splits[0], (ROWS, ROW_LEN, D), 1.0, 6.0, ((0, 16), (1, 2)), (0, 2, 16, 2.0)),
        "segments": draw_segments(jax.random.fold_in(splits[22], 71), 0),
        "pad_mask": draw_pad_mask(jax.random.fold_in(splits[22], 71), 0),
        "dest_shard": draw_dest_shard(jax.random.fold_in(splits[22], 71), 0),
        "dest_slot": draw_dest_slot(jax.random.fold_in(splits[22], 71), 0),
        "ln1_gain": jnp.clip(1.0 + 0.1 * jax.random.normal(splits[5], (D,), jnp.float32), 0.5, 1.5).astype(jnp.bfloat16),
        "ln1_bias": gaussian(splits[6], (D,), 0.3, 1.796875, ((0, 32),)),
        "qkv_weight": gaussian(splits[7], (D, 3 * D), D ** -0.5, 0.1875, ((0, 32),)),
        "qv_bias": gaussian(splits[8], (2, D), 0.5, 3.0, ((1, 32),)),
        "out_weight": gaussian(splits[9], (D, D), (D // 64) ** -0.5, 1.5, ((0, 32),)),
        "out_bias": gaussian(splits[10], (D,), 0.3, 1.796875, ((0, 32),)),
        "ln2_gain": jnp.clip(1.0 + 0.1 * jax.random.normal(splits[11], (D,), jnp.float32), 0.5, 1.5).astype(jnp.bfloat16),
        "ln2_bias": gaussian(splits[12], (D,), 0.3, 1.796875, ((0, 32),)),
        "fc1_weight": gaussian(splits[13], (D, FF), D ** -0.5, 0.1875, ((0, 32),)),
        "fc1_bias": gaussian(splits[14], (FF,), 0.5, 3.0, ((0, 32),)),
        "fc2_weight": gaussian(splits[15], (FF, D), FF ** -0.5, 0.09375, ((0, 32),)),
        "fc2_bias": gaussian(splits[16], (D,), 0.3, 1.796875, ((0, 32),)),
        "learn_gain": jnp.clip(1.0 + 0.1 * jax.random.normal(splits[17], (D,), jnp.float32), 0.5, 1.5).astype(jnp.bfloat16),
        "learn_bias": gaussian(splits[18], (D,), 0.3, 1.796875),
        "maps_weight": gaussian(splits[19], (NTOK, D), D ** -0.5, 0.1875),
        "maps_bias": gaussian(splits[20], (NTOK,), 1.0, 4.0),
        "out_grad": gaussian(splits[21], (N_ROWS, N_SEQ * CAP, NTOK, D), 64.0, 384.0, ((0, 16), (1, 2))),
    }


EPSILON = 1e-06
NEGATIVE = -1e+30
HIGHEST = lax.Precision.HIGHEST

@jax.custom_vjp
def low(v):
    return lax.optimization_barrier(v.astype(jnp.bfloat16)).astype(jnp.float32)

@jax.custom_vjp
def low_back(v):
    return v

def low_keep(v):
    return (low(v), None)

def low_pass(kept, grad):
    return (grad,)

def back_keep(v):
    return (v, None)

def back_low(kept, grad):
    return (low(grad),)
low.defvjp(low_keep, low_pass)
low_back.defvjp(back_keep, back_low)

def product(former, latter):
    return jnp.dot(former, latter, precision=HIGHEST, preferred_element_type=jnp.float32)

def layer_norm(values, scale_vec, shift_vec):
    centred = values - lax.optimization_barrier(jnp.mean(values, axis=-1, keepdims=True))
    variance = lax.optimization_barrier(jnp.mean(centred * centred, axis=-1, keepdims=True))
    return centred * lax.rsqrt(variance + EPSILON) * scale_vec + shift_vec

def row_pools(params, row_tokens, row_ids, row_mask):
    norm1_gain, norm1_shift, qkv_full, qv_full, out_full, out_shift, norm2_gain, norm2_shift, fc1_full, fc1_shift, fc2_full, fc2_shift, learn_scale, learn_shift, map_weight, map_shift = params
    length = row_tokens.shape[0]
    head_count = D // HEAD_DIM
    attn_in = low(layer_norm(row_tokens, norm1_gain, norm1_shift))
    qkv_out = product(attn_in, qkv_full)
    queries = low(low_back(qkv_out[:, :D] + qv_full[0])).reshape(length, head_count, HEAD_DIM)
    key_vecs = low(low_back(qkv_out[:, D:2 * D])).reshape(length, head_count, HEAD_DIM)
    value_vecs = low(low_back(qkv_out[:, 2 * D:] + qv_full[1])).reshape(length, head_count, HEAD_DIM)
    scores = jnp.einsum('qhe,khe->hqk', queries, key_vecs, precision=HIGHEST) * HEAD_DIM ** (-0.5)
    scores = low_back(scores)
    allowed = (row_ids[:, None] == row_ids[None, :])[None]
    scores = jnp.where(allowed, scores, NEGATIVE)
    exponent = jnp.exp(scores - lax.optimization_barrier(jnp.max(scores, axis=-1, keepdims=True)))
    probs = exponent / lax.optimization_barrier(jnp.sum(exponent, axis=-1, keepdims=True))
    mixed_out = jnp.einsum('hqk,khe->qhe', low(probs), value_vecs, precision=HIGHEST).reshape(length, D)
    mixed_out = low(low_back(mixed_out))
    resid1 = row_tokens + low_back(product(mixed_out, out_full) + out_shift)
    hidden = low_back(product(low(layer_norm(resid1, norm2_gain, norm2_shift)), fc1_full) + fc1_shift)
    activated = low(low_back(jax.nn.gelu(hidden, approximate=False)))
    resid2 = resid1 + low_back(product(activated, fc2_full) + fc2_shift)
    logits = product(layer_norm(resid2, learn_scale, learn_shift), map_weight.T) + map_shift
    map_vals = jax.nn.sigmoid(logits) * row_mask[:, None]
    select = (row_ids[:, None] == jnp.arange(IMG_ROW, dtype=jnp.int32)[None, :]).astype(jnp.float32)
    token_weights = (select[:, :, None] * map_vals[:, None, :]).reshape(length, IMG_ROW * NTOK)
    return product(token_weights.T, resid2).reshape(IMG_ROW, NTOK, D)

def reference(tokens, segments, pad_mask, dest_shard, dest_slot, ln1_gain, ln1_bias, qkv_weight, qv_bias, out_weight, out_bias, ln2_gain, ln2_bias, fc1_weight, fc1_bias, fc2_weight, fc2_bias, learn_gain, learn_bias, maps_weight, maps_bias, out_grad):
    params = tuple((weight_item.astype(jnp.float32) for weight_item in (ln1_gain, ln1_bias, qkv_weight, qv_bias, out_weight, out_bias, ln2_gain, ln2_bias, fc1_weight, fc1_bias, fc2_weight, fc2_bias, learn_gain, learn_bias, maps_weight, maps_bias)))
    row_mask = pad_mask.astype(jnp.float32)
    record_ids = jnp.arange(IMG_ROW, dtype=jnp.int32)
    counts = lax.optimization_barrier(jnp.sum((segments[:, :, None] == record_ids[None, None, :]).astype(jnp.float32) * row_mask[:, :, None], axis=1))
    divisor = jnp.maximum(counts, 1.0)
    group_ids = jnp.broadcast_to((jnp.arange(ROWS, dtype=jnp.int32) // ROWS_DEV)[:, None], (ROWS, IMG_ROW)).astype(jnp.int32)
    positions = (dest_shard * CAP + dest_slot).astype(jnp.int32)
    pooled_rows = jax.checkpoint(row_pools)

    def forward(inputs, weights):
        row_sums = lax.map(lambda row_item: pooled_rows(weights, row_item[0], row_item[1], row_item[2]), (inputs, segments, row_mask))
        pooled_vals = low(low_back(row_sums) / divisor[:, :, None, None])
        blank_out = jnp.zeros((N_ROWS, N_SEQ * CAP, NTOK, D), jnp.float32)
        return blank_out.at[group_ids, positions].add(pooled_vals)
    result, pullback = jax.vjp(forward, tokens.astype(jnp.float32), params)
    grad_inputs, param_grads = pullback(out_grad.astype(jnp.float32))
    return (result.astype(jnp.bfloat16), grad_inputs, param_grads[0], param_grads[1], param_grads[2], param_grads[3], param_grads[4], param_grads[5], param_grads[6], param_grads[7], param_grads[8], param_grads[9], param_grads[10], param_grads[11], param_grads[12], param_grads[13], param_grads[14], param_grads[15])
```

```python
import jax
import jax.numpy as jnp
from jax import lax
from jax.experimental import pallas as pl
from jax.experimental.pallas import tpu as pltpu
from jax.sharding import PartitionSpec as P

HEAD_DIM = 64
NTOK = 8
IMG_ROW = 10

EPSILON = 1e-06
NEGATIVE = -1e30
HIGH = lax.Precision.HIGH
BF = jnp.bfloat16
F32 = jnp.float32
SWAP = [(0, 1), (1, 0)]


def dot_plain(a, b, precision=None):
    return jnp.dot(a, b, precision=precision, preferred_element_type=F32)


def dot_first(a, b, precision=None):
    return lax.dot_general(
        a, b, (((0,), (0,)), ((), ())), precision=precision, preferred_element_type=F32
    )


def dot_second(a, b, precision=None):
    return lax.dot_general(
        a, b, (((1,), (1,)), ((), ())), precision=precision, preferred_element_type=F32
    )


def norm_stats(values):
    centred = values - jnp.mean(values, axis=-1, keepdims=True)
    inverse = lax.rsqrt(jnp.mean(centred * centred, axis=-1, keepdims=True) + EPSILON)
    return centred * inverse, inverse


def norm_backward(grad_out, normed, inverse, scale_vec):
    grad_unit = grad_out * scale_vec
    grad_in = inverse * (
        grad_unit
        - jnp.mean(grad_unit, axis=-1, keepdims=True)
        - normed * jnp.mean(grad_unit * normed, axis=-1, keepdims=True)
    )
    return (grad_in, jnp.sum(grad_out * normed, axis=0), jnp.sum(grad_out, axis=0))


def factors(count):
    if count == 16:
        return (4, 2, 2)
    if count == 128:
        return (4, 8, 4)
    return (count, 1, 1)


def rotation(dims, place, step):
    pairs = []
    for a in range(dims[0]):
        for b in range(dims[1]):
            for c in range(dims[2]):
                digits = [a, b, c]
                source = (a * dims[1] + b) * dims[2] + c
                digits[place] = (digits[place] + step) % dims[place]
                pairs.append((source, (digits[0] * dims[1] + digits[1]) * dims[2] + digits[2]))
    return pairs


def crossing(dims, place, flip):
    stride = 1
    for size in dims[place + 1 :]:
        stride *= size
    count = dims[0] * dims[1] * dims[2]
    pairs = []
    for source in range(count):
        digit = (source // stride) % dims[place]
        pairs.append((source, source + ((digit ^ flip) - digit) * stride))
    return pairs


class Wires:
    def __init__(self):
        self.count = lax.axis_size("rows")
        self.dims = factors(self.count)
        row = lax.axis_index("rows")
        self.digits = (
            row // (self.dims[1] * self.dims[2]),
            (row // self.dims[2]) % self.dims[1],
            row % self.dims[2],
        )
        self.seq = lax.axis_index("seq")

    def turn(self, value, place, step):
        return lax.ppermute(value, "rows", rotation(self.dims, place, step))

    def swap(self, value):
        return lax.ppermute(value, "seq", SWAP)


def gate(values, hold):
    return lax.optimization_barrier((values, hold))[0]


def place_kernel(n_parts, dims, chunk, half):
    k0, k1, k2 = dims

    def body(where, *refs):
        parts, out = refs[:n_parts], refs[n_parts]
        buf, sem_in, sem_out = refs[n_parts + 1 :]
        came = []
        at = 0
        for other in (0, 1):
            for colour in (0, 1):
                outer, inner = ((1, 2), (2, 1))[colour]
                for late in range(dims[outer]):
                    part = parts[at]
                    at += 1
                    for mid in range(dims[inner]):
                        for top in range(k0):
                            rel = [0, 0, 0]
                            rel[0], rel[inner], rel[outer] = top, mid, late
                            spot = [
                                lax.rem(where[i] - rel[i] + dims[i], dims[i]) for i in range(3)
                            ]
                            seat = lax.rem(where[3] + other, 2)
                            block = ((spot[0] * k1 + spot[1]) * k2 + spot[2]) * 2 + seat
                            start = pl.multiple_of(block * chunk, chunk)
                            span = (pl.ds(start, chunk), pl.ds(colour * half, half))
                            copy = pltpu.make_async_copy(
                                part.at[mid * k0 + top], buf.at[span], sem_in.at[len(came)]
                            )
                            copy.start()
                            came.append((copy, span))
        went = []
        for copy, span in came:
            copy.wait()
            back = pltpu.make_async_copy(buf.at[span], out.at[span], sem_out.at[len(went)])
            back.start()
            went.append(back)
        for back in went:
            back.wait()

    return body


class Gather:
    def __init__(self, wires, shard):
        self.wires, self.shard = wires, shard
        m, n = shard.shape
        self.plain = bool(m % 32 or n % 256)
        self.half = n // 2
        self.flight, self.held, self.sends = (), (), ()
        self.stage = 0

    def step(self, after=()):
        if self.plain:
            return
        wires, stage = self.wires, self.stage
        self.stage += 1
        if stage == 0:
            shard = gate(self.shard, after) if after else self.shard
            self.flight = [wires.turn(shard, 0, r) for r in range(1, wires.dims[0])]
            return
        pairs = ((1, 2), (2, 1))
        if stage == 1:
            tops = [self.shard] + list(self.flight)
            cuts = [
                jnp.stack([t[:, c * self.half : (c + 1) * self.half] for t in tops])
                for c in (0, 1)
            ]
        else:
            cuts = self.held
        if after:
            cuts = gate(cuts, after)
        if stage == 1:
            self.held = self.sends = cuts
            self.got = [
                [wires.turn(cuts[c], pairs[c][1], r) for r in range(1, wires.dims[pairs[c][1]])]
                for c in (0, 1)
            ]
            self.flight = self.got[0] + self.got[1]
        elif stage == 2:
            mids = [jnp.concatenate([cuts[c]] + self.got[c], axis=0) for c in (0, 1)]
            if after:
                mids = gate(mids, after)
            lists = [
                [wires.turn(mids[c], pairs[c][0], r) for r in range(1, wires.dims[pairs[c][0]])]
                for c in (0, 1)
            ]
            self.held, self.sends = (mids, lists), mids
            self.flight = lists[0] + lists[1]
        elif stage == 3:
            mids, lists = cuts
            own = [mids[0]] + lists[0] + [mids[1]] + lists[1]
            self.flight = [wires.swap(p) for p in own]
            self.held = own

    def result(self):
        wires, shard = self.wires, self.shard
        if self.plain:
            return lax.all_gather(shard, ("rows", "seq"), axis=0, tiled=True)
        m, n = shard.shape
        parts = list(self.held) + list(self.flight)
        where = jnp.stack([*wires.digits, wires.seq]).astype(jnp.int32)
        total = wires.count * 2
        return pl.pallas_call(
            place_kernel(len(parts), wires.dims, m, self.half),
            out_shape=jax.ShapeDtypeStruct((m * total, n), shard.dtype),
            grid_spec=pltpu.PrefetchScalarGridSpec(
                num_scalar_prefetch=1,
                grid=(1,),
                in_specs=[pl.BlockSpec(memory_space=pl.ANY)] * len(parts),
                out_specs=pl.BlockSpec(memory_space=pl.ANY),
                scratch_shapes=[
                    pltpu.VMEM((m * total, n), shard.dtype),
                    pltpu.SemaphoreType.DMA((2 * total,)),
                    pltpu.SemaphoreType.DMA((2 * total,)),
                ],
            ),
            name="place",
        )(where, *parts)


def pick(value, index, axis):
    return lax.dynamic_index_in_dim(value, index, axis, keepdims=False)


def total_of(terms):
    wide = [t.astype(F32) for t in terms]
    return sum(wide[1:], wide[0])


class Scatter:
    def __init__(self, wires, grad):
        self.wires, self.grad = wires, grad
        d, n = grad.shape
        self.m = d // (wires.count * 2)
        self.plain = bool(self.m % 32 or n % 256)
        self.half = n // 2
        self.stage = 0
        self.sends = ()
        self.flight = ()

    def fold(self, terms, place, axis):
        wires = self.wires
        size, spot = wires.dims[place], wires.digits[place]
        kept = [pick(t, spot, axis) for t in terms]
        away, got = [], []
        for step in range(1, size):
            index = lax.rem(spot + step, size)
            send = total_of([pick(t, index, axis) for t in terms]).astype(BF)
            away.append(send)
            got.append(wires.turn(send, place, step))
        return away, kept, got

    def step(self):
        if self.plain:
            return
        wires, stage = self.wires, self.stage
        self.stage += 1
        if stage == 0:
            d, n = self.grad.shape
            cut = self.grad.reshape(*wires.dims, 2, self.m, n)
            send = pick(cut, 1 - wires.seq, 3).astype(BF)
            got = wires.swap(send)
            self.sends, self.flight = [send], [got]
            base = [pick(cut, wires.seq, 3), got]
            half = self.half
            self.terms = [[t[..., c * half : (c + 1) * half] for t in base] for c in (0, 1)]
            return
        places = (((2, 2), (1, 1), (0, 0)), ((1, 1), (2, 1), (0, 0)))
        self.sends, self.flight, terms = [], [], []
        for c in (0, 1):
            away, kept, got = self.fold(self.terms[c], *places[c][stage - 1])
            self.sends += away
            self.flight += got
            terms.append(kept + got)
        self.terms = terms

    def result(self):
        if self.plain:
            both = ("rows", "seq")
            return lax.psum_scatter(self.grad.astype(F32), both, scatter_dimension=0, tiled=True)
        return jnp.concatenate([total_of(t) for t in self.terms], axis=1)


def sum_everywhere(wires, value):
    value = value + wires.swap(value)
    for place in (2, 1, 0):
        size = wires.dims[place]
        step = 1
        while step < size:
            value = value + lax.ppermute(value, "rows", crossing(wires.dims, place, step))
            step *= 2
    return value


def attend_kernel(seg_col, seg_row, q_ref, k_ref, v_ref, mixed_ref, log_ref, bias_ref):
    @pl.when(pl.program_id(1) == 0)
    def _():
        bias_ref[...] = jnp.where(seg_col[0] == seg_row[0], 0.0, NEGATIVE)

    scale = HEAD_DIM ** (-0.5)
    mixed = []
    for h in (0, 1):
        span = slice(h * HEAD_DIM, (h + 1) * HEAD_DIM)
        q = q_ref[:, span] * BF(scale)
        scores = dot_second(k_ref[:, span], q) + bias_ref[...]
        largest = jnp.max(scores, axis=0, keepdims=True)
        exponent = jnp.exp(scores - largest)
        summed = jnp.sum(exponent, axis=0, keepdims=True)
        probs = (exponent * (1.0 / summed)).astype(BF)
        mixed.append(dot_first(v_ref[:, span], probs))
        log_ref[0, 0, h : h + 1, :] = largest + jnp.log(summed)
    mixed_ref[...] = jnp.concatenate(mixed, axis=0).T.astype(BF)


def attend(joined, segments, first, pairs):
    rows, length = segments.shape
    lane = 2 * HEAD_DIM
    all_pairs = joined.shape[1] // (3 * lane)

    def block(start):
        return pl.BlockSpec((length, lane), lambda r, h: (r, start + h))

    return pl.pallas_call(
        attend_kernel,
        grid=(rows, pairs),
        in_specs=[
            pl.BlockSpec((1, length, 1), lambda r, h: (r, 0, 0)),
            pl.BlockSpec((1, 1, length), lambda r, h: (r, 0, 0)),
            block(first),
            block(all_pairs + first),
            block(2 * all_pairs + first),
        ],
        out_specs=[block(0), pl.BlockSpec((1, 1, 2, length), lambda r, h: (r, h, 0, 0))],
        out_shape=[
            jax.ShapeDtypeStruct((rows * length, pairs * lane), BF),
            jax.ShapeDtypeStruct((rows, pairs, 2, length), F32),
        ],
        scratch_shapes=[pltpu.VMEM((length, length), F32)],
        name="attend",
    )(segments[:, :, None], segments[:, None, :], joined, joined, joined)


def attend_back_kernel(
    seg_col, seg_row, q_ref, k_ref, v_ref, log_ref, do_ref, dq_ref, dk_ref, dv_ref, bias_ref
):
    @pl.when(pl.program_id(1) == 0)
    def _():
        bias_ref[...] = jnp.where(seg_col[0] == seg_row[0], 0.0, NEGATIVE)

    scale = HEAD_DIM ** (-0.5)
    grads = []
    for h in (0, 1):
        span = slice(h * HEAD_DIM, (h + 1) * HEAD_DIM)
        q = q_ref[:, span] * BF(scale)
        k = k_ref[:, span]
        do = do_ref[:, span]
        scores = dot_second(k, q) + bias_ref[...]
        probs = jnp.exp(scores - log_ref[0, 0, h : h + 1, :])
        grad_probs = dot_second(v_ref[:, span], do)
        inner = jnp.sum(probs * grad_probs, axis=0, keepdims=True)
        grad_scores = (probs * (grad_probs - inner)).astype(BF)
        dv_ref[:, span] = dot_plain(probs.astype(BF), do).astype(BF)
        dk_ref[:, span] = dot_plain(grad_scores, q).astype(BF)
        grads.append(dot_first(k, grad_scores) * scale)
    dq_ref[...] = jnp.concatenate(grads, axis=0).T.astype(BF)


def attend_back(joined, logs, grad_mixed, segments, first, pairs):
    rows, length = segments.shape
    lane = 2 * HEAD_DIM
    all_pairs = joined.shape[1] // (3 * lane)

    def block(start):
        return pl.BlockSpec((length, lane), lambda r, h: (r, start + h))

    out = jax.ShapeDtypeStruct((rows * length, pairs * lane), BF)
    return pl.pallas_call(
        attend_back_kernel,
        grid=(rows, pairs),
        in_specs=[
            pl.BlockSpec((1, length, 1), lambda r, h: (r, 0, 0)),
            pl.BlockSpec((1, 1, length), lambda r, h: (r, 0, 0)),
            block(first),
            block(all_pairs + first),
            block(2 * all_pairs + first),
            pl.BlockSpec((1, 1, 2, length), lambda r, h: (r, h, 0, 0)),
            block(first),
        ],
        out_specs=[block(0), block(0), block(0)],
        out_shape=[out, out, out],
        scratch_shapes=[pltpu.VMEM((length, length), F32)],
        name="attend_back",
    )(segments[:, :, None], segments[:, None, :], joined, joined, joined, logs, grad_mixed)


def exact_gelu(values):
    return jax.nn.gelu(values, approximate=False)


def shards(
    tokens,
    segments,
    pad_mask,
    dest_shard,
    dest_slot,
    ln1_gain,
    ln1_bias,
    qkv_weight,
    qv_bias,
    out_weight,
    out_bias,
    ln2_gain,
    ln2_bias,
    fc1_weight,
    fc1_bias,
    fc2_weight,
    fc2_bias,
    learn_gain,
    learn_bias,
    maps_weight,
    maps_bias,
    out_grad,
):
    wires = Wires()
    seq = wires.seq
    rows_all, slots_half, width = tokens.shape
    ff = fc1_bias.shape[0] * wires.count * 2
    devices = wires.count * 2
    m = width // devices
    wide = ff // width
    rows_here = rows_all // 2
    row_len = slots_half * 2
    count_tok = rows_here * row_len
    records = rows_here * IMG_ROW
    capacity = out_grad.shape[1]

    small = jnp.concatenate(
        [
            ln1_gain[None],
            ln1_bias[None],
            qv_bias,
            out_bias[None],
            ln2_gain[None],
            ln2_bias[None],
            fc2_bias[None],
            fc1_bias.reshape(wide, m),
        ],
        axis=0,
    )
    n_small = small.shape[0]
    pad_cols = 256
    riding = jnp.concatenate(
        [qkv_weight, jnp.pad(small.T, ((0, 0), (0, pad_cols - n_small)))], axis=1
    )

    def other_rows(value):
        return lax.dynamic_slice_in_dim(value, (1 - seq) * rows_here, rows_here, 0)

    def own_rows(value):
        return lax.dynamic_slice_in_dim(value, seq * rows_here, rows_here, 0)

    came = wires.swap(other_rows(tokens))
    mine = own_rows(tokens)
    first = jnp.where(seq == 0, mine, came)
    second = jnp.where(seq == 0, came, mine)
    inputs_low = jnp.concatenate([first, second], axis=1).reshape(count_tok, width)
    grad_came = wires.swap(out_grad)
    ga, gb, gc, gd = [Gather(wires, w) for w in (riding, out_weight, fc1_weight, fc2_weight)]
    ga.step()
    top_a = ga.flight
    ga.step()
    gb.step(top_a)
    gc.step(gb.flight)
    mid_a = ga.flight
    ga.step()
    gd.step(gc.flight)
    gb.step(mid_a)
    late_a = ga.flight
    ga.step()
    gb.step(late_a)
    qkv_all = ga.result()
    qkv_full = qkv_all[:, : 3 * width]
    small_full = qkv_all[:, 3 * width : 3 * width + 128].T[:n_small].astype(F32)
    norm1_gain, norm1_shift, q_shift, v_shift, out_shift, norm2_gain, norm2_shift, fc2_shift = [
        small_full[i] for i in range(8)
    ]
    fc1_shift = small_full[8:n_small].reshape(wide, devices, m).transpose(1, 0, 2).reshape(ff)
    seg = own_rows(segments)
    seg_flat = seg.reshape(count_tok)
    mask = (seg_flat >= 0).astype(F32)

    inputs = inputs_low.astype(F32)
    normed1, inverse1 = norm_stats(inputs)
    attn_in = (normed1 * norm1_gain + norm1_shift).astype(BF)
    qkv_out = dot_plain(attn_in, qkv_full)
    joined_shift = jnp.concatenate([q_shift, jnp.zeros_like(q_shift), v_shift])
    joined = (qkv_out + joined_shift).astype(BF)
    pairs = width // (4 * HEAD_DIM)
    gb.step()
    gc.step(gb.flight)
    joined = gate(joined, gc.sends)
    mixed_a, logs_a = attend(joined, seg, 0, pairs)
    out_full = gb.result()
    gc.step((mixed_a,))
    joined_b = gate(joined, (gc.sends, mixed_a))
    mixed_b, logs_b = attend(joined_b, seg, pairs, pairs)
    mixed = jnp.concatenate([mixed_a, mixed_b], axis=1)
    resid1 = inputs + dot_plain(mixed, out_full) + out_shift
    normed2, inverse2 = norm_stats(resid1)
    mlp_in = (normed2 * norm2_gain + norm2_shift).astype(BF)
    gc.step()
    gd.step(gc.flight)
    fc1_full = gc.result()
    fc1_full = gate(fc1_full, gd.sends)
    hidden = dot_plain(mlp_in, fc1_full) + fc1_shift
    gd.step()
    gd.step()
    fc2_full = gd.result()
    activated, gelu_back = jax.vjp(exact_gelu, hidden)
    activated_low = activated.astype(BF)
    resid2 = resid1 + dot_plain(activated_low, fc2_full) + fc2_shift

    learn_scale = learn_gain.astype(F32)
    normed3, inverse3 = norm_stats(resid2)
    normed3_out = normed3 * learn_scale + learn_bias.astype(F32)
    map_weight = maps_weight.astype(F32)
    logits = dot_second(normed3_out, map_weight, HIGH) + maps_bias.astype(F32)
    sigmas = jax.nn.sigmoid(logits)
    map_vals = sigmas * mask[:, None]
    row_index = jnp.arange(count_tok, dtype=jnp.int32) // row_len
    owner = jnp.where(seg_flat >= 0, row_index * IMG_ROW + seg_flat, -1)
    select = (owner[:, None] == jnp.arange(records, dtype=jnp.int32)[None, :]).astype(F32)
    token_weights = (select[:, :, None] * map_vals[:, None, :]).reshape(count_tok, records * NTOK)
    sums = dot_first(token_weights, resid2, HIGH)
    counts = jnp.sum(select * mask[:, None], axis=0)
    divisor = jnp.maximum(counts, 1.0)
    positions = own_rows(dest_shard * capacity + dest_slot).reshape(records)
    routing = (
        (positions[None, :] == jnp.arange(2 * capacity, dtype=jnp.int32)[:, None])
        & (counts > 0.0)[None, :]
    ).astype(BF)
    pooled_here = (sums.reshape(records, NTOK * width) / divisor[:, None]).astype(BF)
    pooled_all = dot_plain(routing, pooled_here).astype(BF).reshape(2, capacity, NTOK * width)
    pooled_came = wires.swap(pick(pooled_all, 1 - seq, 0))
    pooled = (pick(pooled_all, seq, 0).astype(F32) + pooled_came.astype(F32)).astype(BF)
    pooled = pooled.reshape(1, capacity, NTOK, width)

    grad_own = out_grad.reshape(capacity, NTOK * width)
    grad_far = grad_came.reshape(capacity, NTOK * width)
    grad_pos = jnp.where(
        seq == 0,
        jnp.concatenate([grad_own, grad_far], axis=0),
        jnp.concatenate([grad_far, grad_own], axis=0),
    )
    grad_records = (dot_first(routing, grad_pos) / divisor[:, None]).astype(BF)
    grad_records = grad_records.reshape(records * NTOK, width).astype(F32)

    grad_resid2 = dot_plain(token_weights, grad_records, HIGH)
    grad_maps_all = dot_second(resid2, grad_records, HIGH).reshape(count_tok, records, NTOK)
    grad_map_vals = jnp.sum(grad_maps_all * select[:, :, None], axis=1)
    grad_logits = grad_map_vals * mask[:, None] * sigmas * (1.0 - sigmas)
    grad_maps_weight = dot_first(grad_logits, normed3_out, HIGH)
    grad_maps_bias = jnp.sum(grad_logits, axis=0)
    grad_normed3 = dot_plain(grad_logits, map_weight, HIGH)
    back_three, grad_learn_gain, grad_learn_bias = norm_backward(
        grad_normed3, normed3, inverse3, learn_scale
    )
    grad_resid2 = grad_resid2 + back_three
    grad_branch2 = grad_resid2.astype(BF)
    s_fc2 = Scatter(wires, dot_first(activated_low, grad_branch2).astype(BF))
    s_fc2.step()
    grad_branch2 = gate(grad_branch2, s_fc2.sends)
    grad_fc2_shift = jnp.sum(grad_branch2.astype(F32), axis=0)
    grad_activ = dot_second(grad_branch2, fc2_full).astype(BF)
    grad_hidden = gelu_back(grad_activ.astype(F32))[0].astype(BF)
    s_fc2.step()
    grad_hidden = gate(grad_hidden, s_fc2.sends)
    s_fc1 = Scatter(wires, dot_first(mlp_in, grad_hidden).astype(BF))
    s_fc1.step()
    grad_hidden = gate(grad_hidden, s_fc1.sends)
    grad_fc1_shift = jnp.sum(grad_hidden.astype(F32), axis=0)
    grad_normed2 = dot_second(grad_hidden, fc1_full)
    back_two, grad_norm2_gain, grad_norm2_shift = norm_backward(
        grad_normed2, normed2, inverse2, norm2_gain
    )
    grad_resid1 = grad_resid2 + back_two
    grad_branch1 = grad_resid1.astype(BF)
    s_fc2.step()
    grad_branch1 = gate(grad_branch1, s_fc2.sends)
    s_out = Scatter(wires, dot_first(mixed, grad_branch1).astype(BF))
    s_out.step()
    grad_out_shift = jnp.sum(grad_branch1.astype(F32), axis=0)
    grad_branch1 = gate(grad_branch1, s_out.sends)
    grad_mixed = dot_second(grad_branch1, out_full).astype(BF)
    s_fc1.step()
    s_fc2.step()
    grad_mixed = gate(grad_mixed, (s_fc1.sends, s_fc2.sends))
    early = jnp.concatenate(
        [
            jnp.stack(
                [
                    grad_learn_gain,
                    grad_learn_bias,
                    grad_out_shift,
                    grad_norm2_gain,
                    grad_norm2_shift,
                    grad_fc2_shift,
                    jnp.pad(grad_maps_bias, (0, width - NTOK)),
                ]
            ),
            grad_maps_weight,
            grad_fc1_shift.reshape(wide, width),
        ],
        axis=0,
    )
    early = sum_everywhere(wires, jnp.pad(early, ((0, -early.shape[0] % 8), (0, 0))))
    dq_a, dk_a, dv_a = attend_back(joined, logs_a, grad_mixed, seg, 0, pairs)
    grad_a = jnp.concatenate([dq_a, dk_a, dv_a], axis=1)
    s_a = Scatter(wires, dot_first(attn_in, grad_a).astype(BF))
    s_a.step()
    s_fc1.step()
    s_out.step()
    grad_mixed = gate(grad_mixed, (s_a.sends, s_fc1.sends, s_out.sends))
    dq_b, dk_b, dv_b = attend_back(joined, logs_b, grad_mixed, seg, pairs, pairs)
    grad_b = jnp.concatenate([dq_b, dk_b, dv_b], axis=1)
    s_a.step()
    s_out.step()
    s_fc1.step()
    done_fc2 = s_fc2.result()
    grad_b = gate(grad_b, (s_a.sends, s_out.sends, s_fc1.sends, done_fc2))
    s_b = Scatter(wires, dot_first(attn_in, grad_b).astype(BF))
    s_b.step()
    s_a.step()
    s_out.step()
    grad_a, grad_b = gate((grad_a, grad_b), (s_a.sends, s_out.sends, s_b.sends, early))
    half = pairs * 2 * HEAD_DIM
    cuts = [slice(i * width + c * half, i * width + (c + 1) * half) for c in (0, 1) for i in range(3)]
    grad_normed1 = sum(
        dot_second(g, jnp.concatenate([qkv_full[:, c] for c in cuts[3 * i : 3 * i + 3]], axis=1))
        for i, g in enumerate((grad_a, grad_b))
    )
    s_b.step()
    grad_normed1 = gate(grad_normed1, s_b.sends)
    back_one, grad_norm1_gain, grad_norm1_shift = norm_backward(
        grad_normed1, normed1, inverse1, norm1_gain
    )
    sum_q, sum_v = [
        jnp.concatenate(
            [jnp.sum(g[:, i * half : (i + 1) * half].astype(F32), axis=0) for g in (grad_a, grad_b)]
        )
        for i in (0, 2)
    ]
    late = jnp.stack([grad_norm1_gain, grad_norm1_shift, sum_q, sum_v])
    late = sum_everywhere(wires, jnp.pad(late, ((0, 4), (0, 0))))
    s_a.step()
    s_b.step()
    s_b.step()
    done_a, done_b = s_a.result(), s_b.result()
    done_out, done_fc1 = s_out.result(), s_fc1.result()
    done_qkv = jnp.concatenate(
        [d[:, i * half : (i + 1) * half] for i in range(3) for d in (done_a, done_b)], axis=1
    )
    place = lax.axis_index("rows") * 2 + seq
    held = lax.dynamic_slice_in_dim(jnp.concatenate([early[2:6], late[:4]]), place * m, m, 1)
    held_fc1 = lax.dynamic_slice_in_dim(
        early[7 + NTOK : 7 + NTOK + wide].reshape(ff), place * wide * m, wide * m, 0
    )
    grad_rows = (grad_resid1 + back_one).reshape(rows_here, row_len, width)
    grad_away = lax.dynamic_slice_in_dim(grad_rows, (1 - seq) * slots_half, slots_half, 1)
    grad_back = wires.swap(grad_away)
    grad_kept = lax.dynamic_slice_in_dim(grad_rows, seq * slots_half, slots_half, 1)
    grad_held = jnp.where(
        seq == 0,
        jnp.concatenate([grad_kept, grad_back], axis=0),
        jnp.concatenate([grad_back, grad_kept], axis=0),
    )
    return (
        pooled,
        grad_held,
        held[4],
        held[5],
        done_qkv,
        held[6:8],
        done_out,
        held[0],
        held[1],
        held[2],
        done_fc1,
        held_fc1,
        done_fc2,
        held[3],
        early[0],
        early[1],
        early[7 : 7 + NTOK],
        early[6, :NTOK],
    )


def solution(mesh):
    both = ("rows", "seq")
    in_specs = (
        P("rows", "seq", None),
        P("rows", None),
        P("rows", "seq"),
        P("rows", None),
        P("rows", None),
        P(both),
        P(both),
        P(both, None),
        P(None, both),
        P(both, None),
        P(both),
        P(both),
        P(both),
        P(both, None),
        P(both),
        P(both, None),
        P(both),
        P(),
        P(),
        P(),
        P(),
        P("rows", "seq", None, None),
    )
    out_specs = (
        P("rows", "seq", None, None),
        P("rows", "seq", None),
        P(both),
        P(both),
        P(both, None),
        P(None, both),
        P(both, None),
        P(both),
        P(both),
        P(both),
        P(both, None),
        P(both),
        P(both, None),
        P(both),
        P(),
        P(),
        P(),
        P(),
    )
    return jax.shard_map(shards, mesh=mesh, in_specs=in_specs, out_specs=out_specs, check_vma=False)
```

```python
import jax
import jax.numpy as jnp
from jax import lax
from jax.experimental import pallas as pl
from jax.experimental.pallas import tpu as pltpu
from jax.sharding import PartitionSpec as P

HEAD_DIM = 64
NTOK = 8
IMG_ROW = 10

EPSILON = 1e-06
NEGATIVE = -1e30
HIGH = lax.Precision.HIGH
BF = jnp.bfloat16
F32 = jnp.float32
SWAP = [(0, 1), (1, 0)]


def dot_plain(a, b, precision=None):
    return jnp.dot(a, b, precision=precision, preferred_element_type=F32)


def dot_first(a, b, precision=None):
    return lax.dot_general(
        a, b, (((0,), (0,)), ((), ())), precision=precision, preferred_element_type=F32
    )


def dot_second(a, b, precision=None):
    return lax.dot_general(
        a, b, (((1,), (1,)), ((), ())), precision=precision, preferred_element_type=F32
    )


def norm_stats(values):
    centred = values - jnp.mean(values, axis=-1, keepdims=True)
    inverse = lax.rsqrt(jnp.mean(centred * centred, axis=-1, keepdims=True) + EPSILON)
    return centred * inverse, inverse


def norm_backward(grad_out, normed, inverse, scale_vec):
    grad_unit = grad_out * scale_vec
    grad_in = inverse * (
        grad_unit
        - jnp.mean(grad_unit, axis=-1, keepdims=True)
        - normed * jnp.mean(grad_unit * normed, axis=-1, keepdims=True)
    )
    return (grad_in, jnp.sum(grad_out * normed, axis=0), jnp.sum(grad_out, axis=0))


def factors(count):
    if count == 16:
        return (4, 2, 2)
    if count == 128:
        return (4, 8, 4)
    return (count, 1, 1)


def rotation(dims, steps):
    pairs = []
    for a in range(dims[0]):
        for b in range(dims[1]):
            for c in range(dims[2]):
                up = [(d + s) % size for d, s, size in zip((a, b, c), steps, dims)]
                source = (a * dims[1] + b) * dims[2] + c
                pairs.append((source, (up[0] * dims[1] + up[1]) * dims[2] + up[2]))
    return pairs


def crossing(dims, place, flip):
    stride = 1
    for size in dims[place + 1 :]:
        stride *= size
    count = dims[0] * dims[1] * dims[2]
    pairs = []
    for source in range(count):
        digit = (source // stride) % dims[place]
        pairs.append((source, source + ((digit ^ flip) - digit) * stride))
    return pairs


class Wires:
    def __init__(self):
        self.count = lax.axis_size("rows")
        self.dims = factors(self.count)
        row = lax.axis_index("rows")
        self.digits = (
            row // (self.dims[1] * self.dims[2]),
            (row // self.dims[2]) % self.dims[1],
            row % self.dims[2],
        )
        self.seq = lax.axis_index("seq")
        self.where = jnp.stack([*self.digits, self.seq]).astype(jnp.int32)

        self.planes = [(y, x) for y in range(self.dims[1]) for x in range(self.dims[2])]

    def turn(self, value, z, y, x):
        return lax.ppermute(value, "rows", rotation(self.dims, (z, y, x)))

    def swap(self, value):
        return lax.ppermute(value, "seq", SWAP)


def gate(values, hold):
    return lax.optimization_barrier((values, hold))[0]


def spans(widths, low, high):
    found, start = [], 0
    for i, width in enumerate(widths):
        a, b = max(low, start), min(high, start + width)
        if a < b:
            found.append((i, a - start, b - start, a))
        start += width
    return found


def stack_kernel(*refs):
    for i, ref in enumerate(refs[:-1]):
        refs[-1][i] = ref[...]


def place_kernel(n_parts, dims, chunk, widths):
    k0, k1, k2 = dims
    planes = [(y, x) for y in range(k1) for x in range(k2)]

    def body(where, *refs):
        parts, outs = refs[:n_parts], refs[n_parts : n_parts + len(widths)]
        buf, sem_in, sem_out = refs[n_parts + len(widths) :]
        came = []
        for other in (0, 1):
            for i, (y, x) in enumerate(planes):
                part = parts[other * len(planes) + i]
                for z in range(k0):
                    spot = [
                        lax.rem(where[j] - r + dims[j], dims[j]) for j, r in enumerate((z, y, x))
                    ]
                    seat = lax.rem(where[3] + other, 2)
                    block = ((spot[0] * k1 + spot[1]) * k2 + spot[2]) * 2 + seat
                    rows = pl.ds(pl.multiple_of(block * chunk, chunk), chunk)
                    copy = pltpu.make_async_copy(part.at[z], buf.at[rows], sem_in.at[len(came)])
                    copy.start()
                    came.append((copy, rows))
        went = []
        for copy, rows in came:
            copy.wait()
            start = 0
            for out, width in zip(outs, widths):
                back = pltpu.make_async_copy(
                    buf.at[rows, pl.ds(start, width)], out.at[rows], sem_out.at[len(went)]
                )
                back.start()
                went.append(back)
                start += width
        for back in went:
            back.wait()

    return body


class Gather:
    def __init__(self, wires, shards):
        self.wires, self.shards = wires, shards
        self.widths = [s.shape[1] for s in shards]
        m, n = shards[0].shape[0], sum(self.widths)
        self.plain = bool(m % 32 or n % 128)
        self.flight, self.sends = (), ()
        self.stage = 0
        if not self.plain:
            self.shard = jnp.concatenate(shards, axis=1) if len(shards) > 1 else shards[0]

    def step(self, after=()):
        if self.plain:
            return
        wires, stage = self.wires, self.stage
        self.stage += 1
        if stage == 0:
            sends = [self.shard]
        elif stage == 1:
            tops = [self.shard, *self.flight]
            out = jax.ShapeDtypeStruct((len(tops), *self.shard.shape), self.shard.dtype)
            sends = [pl.pallas_call(stack_kernel, out_shape=out, name="stack")(*tops)]
        else:
            sends = [self.held, *self.flight]
        if after:
            sends = gate(sends, after)
        if stage == 0:
            self.flight = [wires.turn(sends[0], r, 0, 0) for r in range(1, wires.dims[0])]
        elif stage == 1:
            (self.held,) = sends
            self.flight = [wires.turn(sends[0], 0, y, x) for y, x in wires.planes[1:]]
        else:
            self.held = sends
            self.flight = [wires.swap(p) for p in sends]
        self.sends = sends

    def result(self):
        wires = self.wires
        if self.plain:
            both = ("rows", "seq")
            return [lax.all_gather(s, both, axis=0, tiled=True) for s in self.shards]
        m, n = self.shard.shape
        kind = self.shard.dtype
        parts = [*self.held, *self.flight]
        total = wires.count * 2
        return pl.pallas_call(
            place_kernel(len(parts), wires.dims, m, self.widths),
            out_shape=[jax.ShapeDtypeStruct((m * total, w), kind) for w in self.widths],
            grid_spec=pltpu.PrefetchScalarGridSpec(
                num_scalar_prefetch=1,
                grid=(1,),
                in_specs=[pl.BlockSpec(memory_space=pl.ANY)] * len(parts),
                out_specs=[pl.BlockSpec(memory_space=pl.ANY)] * len(self.widths),
                scratch_shapes=[
                    pltpu.VMEM((m * total, n), kind),
                    pltpu.SemaphoreType.DMA((total,)),
                    pltpu.SemaphoreType.DMA((len(self.widths) * total,)),
                ],
            ),
            name="place",
        )(wires.where, *parts)


def total_of(terms):
    wide = [t.astype(F32) for t in terms]
    return sum(wide[1:], wide[0])


def halves(wires, values):
    width = values.shape[1]
    m = width // (wires.count * 2)
    column = jnp.arange(width, dtype=jnp.int32)
    inside = column % (width // 2)
    seat = jnp.where(column < width // 2, wires.seq, 1 - wires.seq)
    source = (inside // m * 2 + seat) * m + inside % m
    chosen = (jnp.arange(width, dtype=jnp.int32)[:, None] == source[None, :]).astype(BF)
    both = dot_plain(values, chosen).astype(BF)
    return both[:, : width // 2], both[:, width // 2 :]


def inner_fold_kernel(dims, widths):
    n = len(widths)

    def body(where, *refs):
        for at, (up, right) in enumerate(
            (a, b) for a in range(dims[1]) for b in range(dims[2])
        ):
            y = lax.rem(where[1] + up, dims[1])
            x = lax.rem(where[2] + right, dims[2])
            start = 0
            for i, width in enumerate(widths):
                kept, came = refs[i][0, y, x], refs[n + i][0, y, x]
                refs[2 * n + at][0, :, start : start + width] = kept + came
                start += width

    return body


def outer_fold_kernel(dims, n):
    def body(where, *refs):
        for step in range(dims[0]):
            spot = lax.rem(where[0] + step, dims[0])
            refs[n + step][...] = total_of([r[spot] for r in refs[:n]]).astype(BF)

    return body


class Scatter:
    def __init__(self, wires, products):
        self.wires = wires
        self.widths = [p[3].shape[1] for p in products]
        self.m = products[0][0].shape[1] // (wires.count * 2)
        self.plain = bool(self.m % 32 or sum(self.widths) % 128)
        self.stage = 0
        self.sends = ()
        if self.plain:
            self.whole = [dot_first(p[0], p[3]) for p in products]
            return
        shape = (*wires.dims, self.m)
        self.sends = [
            dot_first(p[2], p[3]).astype(BF).reshape(*shape, p[3].shape[1]) for p in products
        ]
        right = gate([p[3] for p in products], self.sends)
        self.kept = [
            dot_first(p[1], r).astype(BF).reshape(*shape, r.shape[1])
            for p, r in zip(products, right)
        ]
        self.got = [wires.swap(s) for s in self.sends]

    def call(self, body, grid, in_specs, out_specs, out_shape, args, name):
        return pl.pallas_call(
            body,
            out_shape=out_shape,
            grid_spec=pltpu.PrefetchScalarGridSpec(
                num_scalar_prefetch=1, grid=grid, in_specs=in_specs, out_specs=out_specs
            ),
            name=name,
        )(self.wires.where, *args)

    def step(self):
        if self.plain:
            return
        wires, stage, m = self.wires, self.stage, self.m
        dims = wires.dims
        k0, k1, k2 = dims
        self.stage += 1
        n = sum(self.widths)
        if stage == 0:
            outs = self.call(
                inner_fold_kernel(dims, self.widths),
                (k0,),
                [pl.BlockSpec((1, k1, k2, m, w), lambda z, p: (z, 0, 0, 0, 0)) for w in self.widths]
                * 2,
                [pl.BlockSpec((1, m, n), lambda z, p: (z, 0, 0))] * (k1 * k2),
                [jax.ShapeDtypeStruct((k0, m, n), BF)] * (k1 * k2),
                [*self.kept, *self.got],
                "fold_inner",
            )
            self.sends = outs[1:]
            self.terms = [outs[0]] + [
                wires.turn(o, 0, y, x) for o, (y, x) in zip(outs[1:], wires.planes[1:])
            ]
        elif stage == 1:
            outs = self.call(
                outer_fold_kernel(dims, len(self.terms)),
                (1,),
                [pl.BlockSpec((k0, m, n), lambda z, p: (0, 0, 0))] * len(self.terms),
                [pl.BlockSpec((m, n), lambda z, p: (0, 0))] * k0,
                [jax.ShapeDtypeStruct((m, n), BF)] * k0,
                self.terms,
                "fold_outer",
            )
            self.sends = outs[1:]
            self.terms = [outs[0]] + [wires.turn(outs[r], r, 0, 0) for r in range(1, k0)]

    def result(self):
        if self.plain:
            both = ("rows", "seq")
            return [lax.psum_scatter(g, both, scatter_dimension=0, tiled=True) for g in self.whole]
        done, outs, start = total_of(self.terms), [], 0
        for w in self.widths:
            outs.append(done[:, start : start + w])
            start += w
        return outs


def pick(value, index, axis):
    return lax.dynamic_index_in_dim(value, index, axis, keepdims=False)


def sum_everywhere(wires, value):
    value = value + wires.swap(value)
    for place in (2, 1, 0):
        size = wires.dims[place]
        step = 1
        while step < size:
            value = value + lax.ppermute(value, "rows", crossing(wires.dims, place, step))
            step *= 2
    return value


def attend_kernel(seg_col, seg_row, q_ref, k_ref, v_ref, mixed_ref, log_ref, bias_ref):
    @pl.when(pl.program_id(1) == 0)
    def _():
        bias_ref[...] = jnp.where(seg_col[0] == seg_row[0], 0.0, NEGATIVE)

    scale = HEAD_DIM ** (-0.5)
    mixed = []
    for h in (0, 1):
        span = slice(h * HEAD_DIM, (h + 1) * HEAD_DIM)
        q = q_ref[:, span] * BF(scale)
        scores = dot_second(k_ref[:, span], q) + bias_ref[...]
        largest = jnp.max(scores, axis=0, keepdims=True)
        exponent = jnp.exp(scores - largest)
        summed = jnp.sum(exponent, axis=0, keepdims=True)
        probs = (exponent * (1.0 / summed)).astype(BF)
        mixed.append(dot_first(v_ref[:, span], probs))
        log_ref[0, 0, h : h + 1, :] = largest + jnp.log(summed)
    mixed_ref[...] = jnp.concatenate(mixed, axis=0).T.astype(BF)


def attend(joined, segments, first, pairs):
    rows, length = segments.shape
    lane = 2 * HEAD_DIM
    all_pairs = joined.shape[1] // (3 * lane)

    def block(start):
        return pl.BlockSpec((length, lane), lambda r, h: (r, start + h))

    return pl.pallas_call(
        attend_kernel,
        grid=(rows, pairs),
        in_specs=[
            pl.BlockSpec((1, length, 1), lambda r, h: (r, 0, 0)),
            pl.BlockSpec((1, 1, length), lambda r, h: (r, 0, 0)),
            block(first),
            block(all_pairs + first),
            block(2 * all_pairs + first),
        ],
        out_specs=[block(0), pl.BlockSpec((1, 1, 2, length), lambda r, h: (r, h, 0, 0))],
        out_shape=[
            jax.ShapeDtypeStruct((rows * length, pairs * lane), BF),
            jax.ShapeDtypeStruct((rows, pairs, 2, length), F32),
        ],
        scratch_shapes=[pltpu.VMEM((length, length), F32)],
        name="attend",
    )(segments[:, :, None], segments[:, None, :], joined, joined, joined)


def attend_back_kernel(
    seg_col, seg_row, q_ref, k_ref, v_ref, log_ref, do_ref, dq_ref, dk_ref, dv_ref, bias_ref
):
    @pl.when(pl.program_id(1) == 0)
    def _():
        bias_ref[...] = jnp.where(seg_col[0] == seg_row[0], 0.0, NEGATIVE)

    scale = HEAD_DIM ** (-0.5)
    grads = []
    for h in (0, 1):
        span = slice(h * HEAD_DIM, (h + 1) * HEAD_DIM)
        q = q_ref[:, span] * BF(scale)
        k = k_ref[:, span]
        do = do_ref[:, span]
        scores = dot_second(k, q) + bias_ref[...]
        probs = jnp.exp(scores - log_ref[0, 0, h : h + 1, :])
        grad_probs = dot_second(v_ref[:, span], do)
        inner = jnp.sum(probs * grad_probs, axis=0, keepdims=True)
        grad_scores = (probs * (grad_probs - inner)).astype(BF)
        dv_ref[:, span] = dot_plain(probs.astype(BF), do).astype(BF)
        dk_ref[:, span] = dot_plain(grad_scores, q).astype(BF)
        grads.append(dot_first(k, grad_scores) * scale)
    dq_ref[...] = jnp.concatenate(grads, axis=0).T.astype(BF)


def attend_back(joined, logs, grad_mixed, segments, first, pairs):
    rows, length = segments.shape
    lane = 2 * HEAD_DIM
    all_pairs = joined.shape[1] // (3 * lane)

    def block(start):
        return pl.BlockSpec((length, lane), lambda r, h: (r, start + h))

    out = jax.ShapeDtypeStruct((rows * length, pairs * lane), BF)
    return pl.pallas_call(
        attend_back_kernel,
        grid=(rows, pairs),
        in_specs=[
            pl.BlockSpec((1, length, 1), lambda r, h: (r, 0, 0)),
            pl.BlockSpec((1, 1, length), lambda r, h: (r, 0, 0)),
            block(first),
            block(all_pairs + first),
            block(2 * all_pairs + first),
            pl.BlockSpec((1, 1, 2, length), lambda r, h: (r, h, 0, 0)),
            block(first),
        ],
        out_specs=[block(0), block(0), block(0)],
        out_shape=[out, out, out],
        scratch_shapes=[pltpu.VMEM((length, length), F32)],
        name="attend_back",
    )(segments[:, :, None], segments[:, None, :], joined, joined, joined, logs, grad_mixed)


ERF_TOP = (
    0.00022905065861350646,
    0.0034082910107109506,
    0.050955695062380861,
    0.18520832239976145,
    1.128379143519084,
)
ERF_LOW = (
    -1.1791602954361697e-7,
    0.000023547966471313185,
    0.0010179625278914885,
    0.014070470171167667,
    0.11098505178285362,
    0.49746925110067538,
    1.0,
)
ROOT_HALF = 0.7071067811865476
ERF_LIMIT = 3.832506856900711 / ROOT_HALF


def polynomial(coefficients, value, outer):
    last = len(coefficients) - 1
    scaled = [c * outer * 0.5 ** (last - i) for i, c in enumerate(coefficients)]
    total = jnp.full_like(value, scaled[0])
    for c in scaled[1:]:
        total = total * value + c
    return total


def gelu_both(values):
    kept = jnp.clip(values, -ERF_LIMIT, ERF_LIMIT)
    square = kept * kept
    top = kept * polynomial(ERF_TOP, square, 0.5 * ROOT_HALF)
    phi = 0.5 + top / polynomial(ERF_LOW, square, 1.0)
    density = jnp.exp2(values * values * -0.7213475204444817 - 1.3257480647361593)
    return values * phi, phi + values * density


def widen_kernel(tile, chunk):
    def body(where, x_ref, w_ref, shift_ref, act_ref, slope_ref, stay_ref, go_ref):
        first = where[3] == 0
        for start in range(0, x_ref.shape[0], tile):
            rows = slice(start, start + tile)
            hidden = dot_plain(x_ref[rows, :], w_ref[...]) + shift_ref[...]
            act, slope = gelu_both(hidden)
            act = act.astype(BF)
            act_ref[rows, :] = act
            slope_ref[rows, :] = slope.astype(BF)
            for i in range(act.shape[1] // (2 * chunk)):
                even = act[:, 2 * i * chunk : (2 * i + 1) * chunk]
                odd = act[:, (2 * i + 1) * chunk : (2 * i + 2) * chunk]
                span = slice(i * chunk, (i + 1) * chunk)
                stay_ref[rows, span] = jnp.where(first, even, odd)
                go_ref[rows, span] = jnp.where(first, odd, even)

    return body


def widen(wires, values, weight, shift):
    count, width = values.shape
    ff = weight.shape[1]
    chunk = ff // (wires.count * 2)
    cols = 512

    def block(size):
        return pl.BlockSpec((count, size), lambda j, p: (0, j))

    out = jax.ShapeDtypeStruct((count, ff), BF)
    part = jax.ShapeDtypeStruct((count, ff // 2), BF)
    return pl.pallas_call(
        widen_kernel(128, chunk),
        out_shape=[out, out, part, part],
        grid_spec=pltpu.PrefetchScalarGridSpec(
            num_scalar_prefetch=1,
            grid=(ff // cols,),
            in_specs=[
                pl.BlockSpec((count, width), lambda j, p: (0, 0)),
                pl.BlockSpec((width, cols), lambda j, p: (0, j)),
                pl.BlockSpec((1, cols), lambda j, p: (0, j)),
            ],
            out_specs=[block(cols), block(cols), block(cols // 2), block(cols // 2)],
        ),
        name="widen",
    )(wires.where, values, weight, shift[None])


def shards(
    tokens,
    segments,
    pad_mask,
    dest_shard,
    dest_slot,
    ln1_gain,
    ln1_bias,
    qkv_weight,
    qv_bias,
    out_weight,
    out_bias,
    ln2_gain,
    ln2_bias,
    fc1_weight,
    fc1_bias,
    fc2_weight,
    fc2_bias,
    learn_gain,
    learn_bias,
    maps_weight,
    maps_bias,
    out_grad,
):
    wires = Wires()
    seq = wires.seq
    rows_all, slots_half, width = tokens.shape
    ff = fc1_bias.shape[0] * wires.count * 2
    devices = wires.count * 2
    m = width // devices
    wide = ff // width
    rows_here = rows_all // 2
    row_len = slots_half * 2
    count_tok = rows_here * row_len
    records = rows_here * IMG_ROW
    capacity = out_grad.shape[1]

    small = jnp.concatenate(
        [
            ln1_gain[None],
            ln1_bias[None],
            qv_bias,
            out_bias[None],
            ln2_gain[None],
            ln2_bias[None],
            fc2_bias[None],
            fc1_bias.reshape(wide, m),
        ],
        axis=0,
    )
    n_small = small.shape[0]
    pad_cols = 256
    small_cols = jnp.pad(small.T, ((0, 0), (0, pad_cols - n_small)))

    def other_rows(value):
        return lax.dynamic_slice_in_dim(value, (1 - seq) * rows_here, rows_here, 0)

    def own_rows(value):
        return lax.dynamic_slice_in_dim(value, seq * rows_here, rows_here, 0)

    came = wires.swap(other_rows(tokens))
    mine = own_rows(tokens)
    first = jnp.where(seq == 0, mine, came)
    second = jnp.where(seq == 0, came, mine)
    inputs_low = jnp.concatenate([first, second], axis=1).reshape(count_tok, width)
    grad_came = wires.swap(out_grad)
    ga = Gather(wires, [qkv_weight, small_cols])
    gc = Gather(wires, [out_weight, fc1_weight])
    gd = Gather(wires, [fc2_weight])
    ga.step()
    gc.step(ga.flight)
    ga.step()
    gd.step(gc.flight)
    gc.step(ga.sends)
    ga.step(gc.sends)
    qkv_full, small_all = ga.result()
    small_full = small_all[:, :128].T[:n_small].astype(F32)
    norm1_gain, norm1_shift, q_shift, v_shift, out_shift, norm2_gain, norm2_shift, fc2_shift = [
        small_full[i] for i in range(8)
    ]
    fc1_shift = small_full[8:n_small].reshape(wide, devices, m).transpose(1, 0, 2).reshape(ff)
    seg = own_rows(segments)
    seg_flat = seg.reshape(count_tok)
    mask = (seg_flat >= 0).astype(F32)

    inputs = inputs_low.astype(F32)
    normed1, inverse1 = norm_stats(inputs)
    attn_in = (normed1 * norm1_gain + norm1_shift).astype(BF)
    qkv_out = dot_plain(attn_in, qkv_full)
    joined_shift = jnp.concatenate([q_shift, jnp.zeros_like(q_shift), v_shift])
    joined = (qkv_out + joined_shift).astype(BF)
    pairs = width // (4 * HEAD_DIM)
    mixed, logs = attend(joined, seg, 0, 2 * pairs)
    gc.step((mixed,))
    gd.step(gc.sends)
    out_full, fc1_full = gc.result()
    mixed = gate(mixed, gd.sends)
    resid1 = inputs + dot_plain(mixed, out_full) + out_shift
    normed2, inverse2 = norm_stats(resid1)
    mlp_in = (normed2 * norm2_gain + norm2_shift).astype(BF)
    activated_low, slope, act_stay, act_go = widen(wires, mlp_in, fc1_full, fc1_shift)
    gd.step((slope,))
    (fc2_full,) = gd.result()
    resid2 = resid1 + dot_plain(activated_low, fc2_full) + fc2_shift

    learn_scale = learn_gain.astype(F32)
    normed3, inverse3 = norm_stats(resid2)
    normed3_out = normed3 * learn_scale + learn_bias.astype(F32)
    map_weight = maps_weight.astype(F32)
    logits = dot_second(normed3_out, map_weight, HIGH) + maps_bias.astype(F32)
    sigmas = jax.nn.sigmoid(logits)
    map_vals = sigmas * mask[:, None]
    row_index = jnp.arange(count_tok, dtype=jnp.int32) // row_len
    owner = jnp.where(seg_flat >= 0, row_index * IMG_ROW + seg_flat, -1)
    select = (owner[:, None] == jnp.arange(records, dtype=jnp.int32)[None, :]).astype(F32)
    token_weights = (select[:, :, None] * map_vals[:, None, :]).reshape(count_tok, records * NTOK)
    sums = dot_first(token_weights, resid2, HIGH)
    counts = jnp.sum(select * mask[:, None], axis=0)
    divisor = jnp.maximum(counts, 1.0)
    positions = own_rows(dest_shard * capacity + dest_slot).reshape(records)
    routing = (
        (positions[None, :] == jnp.arange(2 * capacity, dtype=jnp.int32)[:, None])
        & (counts > 0.0)[None, :]
    ).astype(BF)
    pooled_here = (sums.reshape(records, NTOK * width) / divisor[:, None]).astype(BF)
    pooled_all = dot_plain(routing, pooled_here).astype(BF).reshape(2, capacity, NTOK * width)
    pooled_came = wires.swap(pick(pooled_all, 1 - seq, 0))
    pooled = (pick(pooled_all, seq, 0).astype(F32) + pooled_came.astype(F32)).astype(BF)
    pooled = pooled.reshape(1, capacity, NTOK, width)

    grad_own = out_grad.reshape(capacity, NTOK * width)
    grad_far = grad_came.reshape(capacity, NTOK * width)
    grad_pos = jnp.where(
        seq == 0,
        jnp.concatenate([grad_own, grad_far], axis=0),
        jnp.concatenate([grad_far, grad_own], axis=0),
    )
    grad_records = (dot_first(routing, grad_pos) / divisor[:, None]).astype(BF)
    grad_records = grad_records.reshape(records * NTOK, width).astype(F32)

    grad_resid2 = dot_plain(token_weights, grad_records, HIGH)
    grad_maps_all = dot_second(resid2, grad_records, HIGH).reshape(count_tok, records, NTOK)
    grad_map_vals = jnp.sum(grad_maps_all * select[:, :, None], axis=1)
    grad_logits = grad_map_vals * mask[:, None] * sigmas * (1.0 - sigmas)
    grad_maps_weight = dot_first(grad_logits, normed3_out, HIGH)
    grad_maps_bias = jnp.sum(grad_logits, axis=0)
    grad_normed3 = dot_plain(grad_logits, map_weight, HIGH)
    back_three, grad_learn_gain, grad_learn_bias = norm_backward(
        grad_normed3, normed3, inverse3, learn_scale
    )
    grad_resid2 = grad_resid2 + back_three
    grad_branch2 = grad_resid2.astype(BF)
    s_fc2 = Scatter(wires, [(activated_low, act_stay, act_go, grad_branch2)])
    grad_branch2 = gate(grad_branch2, s_fc2.sends)
    grad_fc2_shift = jnp.sum(grad_branch2.astype(F32), axis=0)
    grad_activ = dot_second(grad_branch2, fc2_full).astype(BF)
    grad_hidden = (grad_activ.astype(F32) * slope.astype(F32)).astype(BF)
    s_fc2.step()
    grad_hidden = gate(grad_hidden, s_fc2.sends)
    s_fc1 = Scatter(wires, [(mlp_in, *halves(wires, mlp_in), grad_hidden)])
    grad_hidden = gate(grad_hidden, s_fc1.sends)
    grad_fc1_shift = jnp.sum(grad_hidden.astype(F32), axis=0)
    grad_normed2 = dot_second(grad_hidden, fc1_full)
    back_two, grad_norm2_gain, grad_norm2_shift = norm_backward(
        grad_normed2, normed2, inverse2, norm2_gain
    )
    grad_resid1 = grad_resid2 + back_two
    grad_branch1 = grad_resid1.astype(BF)
    s_fc1.step()
    s_fc2.step()
    grad_branch1 = gate(grad_branch1, (s_fc1.sends, s_fc2.sends))
    s_out = Scatter(wires, [(mixed, *halves(wires, mixed), grad_branch1)])
    grad_out_shift = jnp.sum(grad_branch1.astype(F32), axis=0)
    grad_branch1 = gate(grad_branch1, s_out.sends)
    grad_mixed = dot_second(grad_branch1, out_full).astype(BF)
    s_out.step()
    grad_mixed = gate(grad_mixed, s_out.sends)
    dq_a, dk_a, dv_a = attend_back(joined, logs[:, :pairs], grad_mixed, seg, 0, pairs)
    grad_a = jnp.concatenate([dq_a, dk_a, dv_a], axis=1)
    attn_stay, attn_go = halves(wires, attn_in)
    s_a = Scatter(wires, [(attn_in, attn_stay, attn_go, grad_a)])
    s_fc1.step()
    grad_mixed = gate(grad_mixed, (s_a.sends, s_fc1.sends))
    dq_b, dk_b, dv_b = attend_back(joined, logs[:, pairs:], grad_mixed, seg, pairs, pairs)
    grad_b = jnp.concatenate([dq_b, dk_b, dv_b], axis=1)
    s_a.step()
    s_out.step()
    (done_fc2,) = s_fc2.result()
    grad_b = gate(grad_b, (s_a.sends, s_out.sends, done_fc2))
    s_b = Scatter(wires, [(attn_in, attn_stay, attn_go, grad_b)])
    grad_a, grad_b = gate((grad_a, grad_b), s_b.sends)
    half = pairs * 2 * HEAD_DIM
    cuts = [slice(i * width + c * half, i * width + (c + 1) * half) for c in (0, 1) for i in range(3)]
    grad_normed1 = sum(
        dot_second(g, jnp.concatenate([qkv_full[:, c] for c in cuts[3 * i : 3 * i + 3]], axis=1))
        for i, g in enumerate((grad_a, grad_b))
    )
    s_b.step()
    grad_normed1 = gate(grad_normed1, s_b.sends)
    back_one, grad_norm1_gain, grad_norm1_shift = norm_backward(
        grad_normed1, normed1, inverse1, norm1_gain
    )
    sum_q, sum_v = [
        jnp.concatenate(
            [jnp.sum(g[:, i * half : (i + 1) * half].astype(F32), axis=0) for g in (grad_a, grad_b)]
        )
        for i in (0, 2)
    ]
    little = jnp.concatenate(
        [
            jnp.stack(
                [
                    grad_norm1_gain,
                    grad_norm1_shift,
                    sum_q,
                    sum_v,
                    grad_out_shift,
                    grad_norm2_gain,
                    grad_norm2_shift,
                    grad_fc2_shift,
                    grad_learn_gain,
                    grad_learn_bias,
                    jnp.pad(grad_maps_bias, (0, width - NTOK)),
                ]
            ),
            grad_maps_weight,
            grad_fc1_shift.reshape(wide, width),
        ],
        axis=0,
    )
    little = sum_everywhere(wires, jnp.pad(little, ((0, -little.shape[0] % 8), (0, 0))))
    s_a.step()
    s_b.step()
    (done_a,), (done_b,) = s_a.result(), s_b.result()
    (done_fc1,), (done_out,) = s_fc1.result(), s_out.result()
    done_qkv = jnp.concatenate(
        [d[:, i * half : (i + 1) * half] for i in range(3) for d in (done_a, done_b)], axis=1
    )
    place = lax.axis_index("rows") * 2 + seq
    held = lax.dynamic_slice_in_dim(little[:8], place * m, m, 1)
    held_fc1 = lax.dynamic_slice_in_dim(
        little[11 + NTOK : 11 + NTOK + wide].reshape(ff), place * wide * m, wide * m, 0
    )
    grad_rows = (grad_resid1 + back_one).reshape(rows_here, row_len, width)
    grad_away = lax.dynamic_slice_in_dim(grad_rows, (1 - seq) * slots_half, slots_half, 1)
    grad_back = wires.swap(grad_away)
    grad_kept = lax.dynamic_slice_in_dim(grad_rows, seq * slots_half, slots_half, 1)
    grad_held = jnp.where(
        seq == 0,
        jnp.concatenate([grad_kept, grad_back], axis=0),
        jnp.concatenate([grad_back, grad_kept], axis=0),
    )
    return (
        pooled,
        grad_held,
        held[0],
        held[1],
        done_qkv,
        held[2:4],
        done_out,
        held[4],
        held[5],
        held[6],
        done_fc1,
        held_fc1,
        done_fc2,
        held[7],
        little[8],
        little[9],
        little[11 : 11 + NTOK],
        little[10, :NTOK],
    )


def solution(mesh):
    both = ("rows", "seq")
    in_specs = (
        P("rows", "seq", None),
        P("rows", None),
        P("rows", "seq"),
        P("rows", None),
        P("rows", None),
        P(both),
        P(both),
        P(both, None),
        P(None, both),
        P(both, None),
        P(both),
        P(both),
        P(both),
        P(both, None),
        P(both),
        P(both, None),
        P(both),
        P(),
        P(),
        P(),
        P(),
        P("rows", "seq", None, None),
    )
    out_specs = (
        P("rows", "seq", None, None),
        P("rows", "seq", None),
        P(both),
        P(both),
        P(both, None),
        P(None, both),
        P(both, None),
        P(both),
        P(both),
        P(both),
        P(both, None),
        P(both),
        P(both, None),
        P(both),
        P(),
        P(),
        P(),
        P(),
    )
    return jax.shard_map(shards, mesh=mesh, in_specs=in_specs, out_specs=out_specs, check_vma=False)
```

```python
import jax
import jax.numpy as jnp
from jax import lax
from jax.experimental import pallas as pl
from jax.experimental.pallas import tpu as pltpu
from jax.sharding import PartitionSpec as P

HEAD_DIM = 64
NTOK = 8
IMG_ROW = 10

EPSILON = 1e-06
NEGATIVE = -1e30
HIGH = lax.Precision.HIGH
BF = jnp.bfloat16
F32 = jnp.float32
SWAP = [(0, 1), (1, 0)]


def dot_plain(a, b, precision=None):
    return jnp.dot(a, b, precision=precision, preferred_element_type=F32)


def dot_first(a, b, precision=None):
    return lax.dot_general(
        a, b, (((0,), (0,)), ((), ())), precision=precision, preferred_element_type=F32
    )


def dot_second(a, b, precision=None):
    return lax.dot_general(
        a, b, (((1,), (1,)), ((), ())), precision=precision, preferred_element_type=F32
    )


def norm_stats(values):
    centred = values - jnp.mean(values, axis=-1, keepdims=True)
    inverse = lax.rsqrt(jnp.mean(centred * centred, axis=-1, keepdims=True) + EPSILON)
    return centred * inverse, inverse


def norm_backward(grad_out, normed, inverse, scale_vec):
    grad_unit = grad_out * scale_vec
    grad_in = inverse * (
        grad_unit
        - jnp.mean(grad_unit, axis=-1, keepdims=True)
        - normed * jnp.mean(grad_unit * normed, axis=-1, keepdims=True)
    )
    return (grad_in, jnp.sum(grad_out * normed, axis=0), jnp.sum(grad_out, axis=0))


def factors(count):
    if count == 16:
        return (4, 2, 2)
    if count == 128:
        return (4, 8, 4)
    return (count, 1, 1)


def rotation(dims, steps):
    pairs = []
    for a in range(dims[0]):
        for b in range(dims[1]):
            for c in range(dims[2]):
                up = [(d + s) % size for d, s, size in zip((a, b, c), steps, dims)]
                source = (a * dims[1] + b) * dims[2] + c
                pairs.append((source, (up[0] * dims[1] + up[1]) * dims[2] + up[2]))
    return pairs


def crossing(dims, flips):
    pairs = []
    for a in range(dims[0]):
        for b in range(dims[1]):
            for c in range(dims[2]):
                other = [d ^ f for d, f in zip((a, b, c), flips)]
                source = (a * dims[1] + b) * dims[2] + c
                pairs.append((source, (other[0] * dims[1] + other[1]) * dims[2] + other[2]))
    return pairs


class Wires:
    def __init__(self):
        self.count = lax.axis_size("rows")
        self.dims = factors(self.count)
        row = lax.axis_index("rows")
        self.digits = (
            row // (self.dims[1] * self.dims[2]),
            (row // self.dims[2]) % self.dims[1],
            row % self.dims[2],
        )
        self.seq = lax.axis_index("seq")
        self.where = jnp.stack([*self.digits, self.seq]).astype(jnp.int32)

        self.planes = [(y, x) for y in range(self.dims[1]) for x in range(self.dims[2])]

    def turn(self, value, z, y, x):
        return lax.ppermute(value, "rows", rotation(self.dims, (z, y, x)))

    def swap(self, value):
        return lax.ppermute(value, "seq", SWAP)


def gate(values, hold):
    return lax.optimization_barrier((values, hold))[0]


def spans(widths, low, high):
    found, start = [], 0
    for i, width in enumerate(widths):
        a, b = max(low, start), min(high, start + width)
        if a < b:
            found.append((i, a - start, b - start, a))
        start += width
    return found


def stack_kernel(*refs):
    for i, ref in enumerate(refs[:-1]):
        refs[-1][i] = ref[...]


def place_kernel(n_parts, dims, chunk, widths):
    k0, k1, k2 = dims
    planes = [(y, x) for y in range(k1) for x in range(k2)]

    def body(where, *refs):
        parts, outs = refs[:n_parts], refs[n_parts : n_parts + len(widths)]
        buf, sem_in, sem_out = refs[n_parts + len(widths) :]
        came = []
        for other in (0, 1):
            for i, (y, x) in enumerate(planes):
                part = parts[other * len(planes) + i]
                for z in range(k0):
                    spot = [
                        lax.rem(where[j] - r + dims[j], dims[j]) for j, r in enumerate((z, y, x))
                    ]
                    seat = lax.rem(where[3] + other, 2)
                    block = ((spot[0] * k1 + spot[1]) * k2 + spot[2]) * 2 + seat
                    rows = pl.ds(pl.multiple_of(block * chunk, chunk), chunk)
                    copy = pltpu.make_async_copy(part.at[z], buf.at[rows], sem_in.at[len(came)])
                    copy.start()
                    came.append((copy, rows))
        went = []
        for copy, rows in came:
            copy.wait()
            start = 0
            for out, width in zip(outs, widths):
                back = pltpu.make_async_copy(
                    buf.at[rows, pl.ds(start, width)], out.at[rows], sem_out.at[len(went)]
                )
                back.start()
                went.append(back)
                start += width
        for back in went:
            back.wait()

    return body


class Gather:
    def __init__(self, wires, shards):
        self.wires, self.shards = wires, shards
        self.widths = [s.shape[1] for s in shards]
        m, n = shards[0].shape[0], sum(self.widths)
        self.plain = bool(m % 32 or n % 128)
        self.flight, self.sends = (), ()
        self.stage = 0
        if not self.plain:
            self.shard = jnp.concatenate(shards, axis=1) if len(shards) > 1 else shards[0]

    def step(self, after=()):
        if self.plain:
            return
        wires, stage = self.wires, self.stage
        self.stage += 1
        if stage == 0:
            sends = [self.shard]
        elif stage == 1:
            tops = [self.shard, *self.flight]
            out = jax.ShapeDtypeStruct((len(tops), *self.shard.shape), self.shard.dtype)
            sends = [pl.pallas_call(stack_kernel, out_shape=out, name="stack")(*tops)]
        else:
            sends = [self.held, *self.flight]
        if after:
            sends = gate(sends, after)
        if stage == 0:
            self.flight = [wires.turn(sends[0], r, 0, 0) for r in range(1, wires.dims[0])]
        elif stage == 1:
            (self.held,) = sends
            self.flight = [wires.turn(sends[0], 0, y, x) for y, x in wires.planes[1:]]
        else:
            self.held = sends
            self.flight = [wires.swap(p) for p in sends]
        self.sends = sends

    def result(self):
        wires = self.wires
        if self.plain:
            both = ("rows", "seq")
            return [lax.all_gather(s, both, axis=0, tiled=True) for s in self.shards]
        m, n = self.shard.shape
        kind = self.shard.dtype
        parts = [*self.held, *self.flight]
        total = wires.count * 2
        return pl.pallas_call(
            place_kernel(len(parts), wires.dims, m, self.widths),
            out_shape=[jax.ShapeDtypeStruct((m * total, w), kind) for w in self.widths],
            grid_spec=pltpu.PrefetchScalarGridSpec(
                num_scalar_prefetch=1,
                grid=(1,),
                in_specs=[pl.BlockSpec(memory_space=pl.ANY)] * len(parts),
                out_specs=[pl.BlockSpec(memory_space=pl.ANY)] * len(self.widths),
                scratch_shapes=[
                    pltpu.VMEM((m * total, n), kind),
                    pltpu.SemaphoreType.DMA((total,)),
                    pltpu.SemaphoreType.DMA((len(self.widths) * total,)),
                ],
            ),
            name="place",
        )(wires.where, *parts)


def total_of(terms):
    wide = [t.astype(F32) for t in terms]
    return sum(wide[1:], wide[0])


def halves(wires, values):
    width = values.shape[1]
    m = width // (wires.count * 2)
    column = jnp.arange(width, dtype=jnp.int32)
    inside = column % (width // 2)
    seat = jnp.where(column < width // 2, wires.seq, 1 - wires.seq)
    source = (inside // m * 2 + seat) * m + inside % m
    chosen = (jnp.arange(width, dtype=jnp.int32)[:, None] == source[None, :]).astype(BF)
    both = dot_plain(values, chosen).astype(BF)
    return both[:, : width // 2], both[:, width // 2 :]


def inner_fold_kernel(dims, widths):
    n = len(widths)

    def body(where, *refs):
        for at, (up, right) in enumerate(
            (a, b) for a in range(dims[1]) for b in range(dims[2])
        ):
            y = lax.rem(where[1] + up, dims[1])
            x = lax.rem(where[2] + right, dims[2])
            start = 0
            for i, width in enumerate(widths):
                kept, came = refs[i][0, y, x], refs[n + i][0, y, x]
                refs[2 * n + at][0, :, start : start + width] = kept + came
                start += width

    return body


def outer_fold_kernel(dims, counts):
    n = sum(counts)

    def body(where, *refs):
        for step in range(dims[0]):
            spot = lax.rem(where[0] + step, dims[0])
            at, start = 0, 0
            for count in counts:
                width = refs[at].shape[2]
                total = total_of([r[spot] for r in refs[at : at + count]]).astype(BF)
                refs[n + step][:, start : start + width] = total
                at += count
                start += width

    return body


def prefetched(wires, body, grid, in_specs, out_specs, out_shape, args, name):
    return pl.pallas_call(
        body,
        out_shape=out_shape,
        grid_spec=pltpu.PrefetchScalarGridSpec(
            num_scalar_prefetch=1, grid=grid, in_specs=in_specs, out_specs=out_specs
        ),
        name=name,
    )(wires.where, *args)


class Scatter:
    def __init__(self, wires):
        self.wires = wires
        self.widths, self.kept, self.got, self.whole, self.terms = [], [], [], [], ()

    def add(self, left, stay, go, right):
        wires = self.wires
        width = right.shape[1]
        self.m = left.shape[1] // (wires.count * 2)
        self.plain = bool(self.m % 32 or width % 512)
        self.widths.append(width)
        if self.plain:
            self.whole.append(dot_first(left, right))
            return ()
        shape = (*wires.dims, self.m, width)
        send = dot_first(go, right).astype(BF).reshape(shape)
        kept = dot_first(stay, gate(right, send)).astype(BF).reshape(shape)
        self.kept.append(kept)
        self.got.append(wires.swap(send))
        return send, kept

    def inner(self):
        if self.plain:
            return ()
        wires, m = self.wires, self.m
        k0, k1, k2 = wires.dims
        n = sum(self.widths)
        outs = prefetched(
            wires,
            inner_fold_kernel(wires.dims, self.widths),
            (k0,),
            [pl.BlockSpec((1, k1, k2, m, w), lambda z, p: (z, 0, 0, 0, 0)) for w in self.widths] * 2,
            [pl.BlockSpec((1, m, n), lambda z, p: (z, 0, 0))] * (k1 * k2),
            [jax.ShapeDtypeStruct((k0, m, n), BF)] * (k1 * k2),
            [*self.kept, *self.got],
            "fold_inner",
        )
        self.terms = [outs[0]] + [
            wires.turn(o, 0, y, x) for o, (y, x) in zip(outs[1:], wires.planes[1:])
        ]
        return outs


class Outer:
    def __init__(self, wires, groups, after=()):
        self.wires, self.groups = wires, groups
        self.plain = groups[0].plain
        if self.plain:
            self.sends = ()
            return
        k0 = wires.dims[0]
        self.tall = max(g.m for g in groups)
        self.steps = 4
        self.rows = min(g.m for g in groups)
        terms = [g.terms for g in groups]
        if after:
            terms = gate(terms, after)
        specs, self.blocks = [], []
        for g in groups:
            width = sum(g.widths)
            if g.m == self.rows:
                self.blocks.append(width // self.steps)
                spec = pl.BlockSpec((k0, g.m, width // self.steps), lambda j, p: (0, 0, j))
            else:
                self.blocks.append(width)
                spec = pl.BlockSpec((k0, self.rows, width), lambda j, p: (0, j, 0))
            specs += [spec] * len(g.terms)
        n = sum(self.blocks)
        outs = prefetched(
            wires,
            outer_fold_kernel(wires.dims, [len(t) for t in terms]),
            (self.steps,),
            specs,
            [pl.BlockSpec((self.rows, n), lambda j, p: (0, j))] * k0,
            [jax.ShapeDtypeStruct((self.rows, n * self.steps), BF)] * k0,
            [t for group in terms for t in group],
            "fold_outer",
        )
        self.sends = outs
        self.terms = [outs[0]] + [wires.turn(outs[r], r, 0, 0) for r in range(1, k0)]

    def result(self, after=()):
        if self.plain:
            both = ("rows", "seq")
            return [
                lax.psum_scatter(w, both, scatter_dimension=0, tiled=True)
                for g in self.groups
                for w in g.whole
            ]
        terms = gate(self.terms, after) if after else self.terms
        done = total_of(terms).reshape(self.rows, self.steps, sum(self.blocks))
        outs, start = [], 0
        for g, block in zip(self.groups, self.blocks):
            part = done[:, :, start : start + block]
            start += block
            if g.m != self.rows:
                outs.append(part.transpose(1, 0, 2).reshape(g.m, block))
                continue
            part, at = part.reshape(self.rows, block * self.steps), 0
            for width in g.widths:
                outs.append(part[:, at : at + width])
                at += width
        return outs


def pick(value, index, axis):
    return lax.dynamic_index_in_dim(value, index, axis, keepdims=False)


def sum_everywhere(wires, value):
    value = value + wires.swap(value)
    dims = wires.dims
    planes = [(0, y, x) for y, x in wires.planes]
    for flips in (planes, [(z, 0, 0) for z in range(dims[0])]):
        terms = [value] + [
            lax.ppermute(value, "rows", crossing(dims, flip)) for flip in flips[1:]
        ]
        while len(terms) > 1:
            terms = [a + b for a, b in zip(terms[::2], terms[1::2])]
        (value,) = terms
    return value


def attend_kernel(seg_col, seg_row, q_ref, k_ref, v_ref, mixed_ref, log_ref, bias_ref):
    @pl.when(pl.program_id(1) == 0)
    def _():
        bias_ref[...] = jnp.where(seg_col[0] == seg_row[0], 0.0, NEGATIVE)

    scale = HEAD_DIM ** (-0.5)
    mixed = []
    for h in (0, 1):
        span = slice(h * HEAD_DIM, (h + 1) * HEAD_DIM)
        q = q_ref[:, span] * BF(scale)
        scores = dot_second(k_ref[:, span], q) + bias_ref[...]
        largest = jnp.max(scores, axis=0, keepdims=True)
        exponent = jnp.exp(scores - largest)
        summed = jnp.sum(exponent, axis=0, keepdims=True)
        probs = (exponent * (1.0 / summed)).astype(BF)
        mixed.append(dot_first(v_ref[:, span], probs))
        log_ref[0, 0, h : h + 1, :] = largest + jnp.log(summed)
    mixed_ref[...] = jnp.concatenate(mixed, axis=0).T.astype(BF)


def attend(joined, segments, first, pairs):
    rows, length = segments.shape
    lane = 2 * HEAD_DIM
    all_pairs = joined.shape[1] // (3 * lane)

    def block(start):
        return pl.BlockSpec((length, lane), lambda r, h: (r, start + h))

    return pl.pallas_call(
        attend_kernel,
        grid=(rows, pairs),
        in_specs=[
            pl.BlockSpec((1, length, 1), lambda r, h: (r, 0, 0)),
            pl.BlockSpec((1, 1, length), lambda r, h: (r, 0, 0)),
            block(first),
            block(all_pairs + first),
            block(2 * all_pairs + first),
        ],
        out_specs=[block(0), pl.BlockSpec((1, 1, 2, length), lambda r, h: (r, h, 0, 0))],
        out_shape=[
            jax.ShapeDtypeStruct((rows * length, pairs * lane), BF),
            jax.ShapeDtypeStruct((rows, pairs, 2, length), F32),
        ],
        scratch_shapes=[pltpu.VMEM((length, length), F32)],
        name="attend",
    )(segments[:, :, None], segments[:, None, :], joined, joined, joined)


def attend_back_kernel(
    seg_col, seg_row, q_ref, k_ref, v_ref, log_ref, do_ref, dq_ref, dk_ref, dv_ref, bias_ref
):
    @pl.when(pl.program_id(1) == 0)
    def _():
        bias_ref[...] = jnp.where(seg_col[0] == seg_row[0], 0.0, NEGATIVE)

    scale = HEAD_DIM ** (-0.5)
    grads = []
    for h in (0, 1):
        span = slice(h * HEAD_DIM, (h + 1) * HEAD_DIM)
        q = q_ref[:, span] * BF(scale)
        k = k_ref[:, span]
        do = do_ref[:, span]
        scores = dot_second(k, q) + bias_ref[...]
        probs = jnp.exp(scores - log_ref[0, 0, h : h + 1, :])
        grad_probs = dot_second(v_ref[:, span], do)
        inner = jnp.sum(probs * grad_probs, axis=0, keepdims=True)
        grad_scores = (probs * (grad_probs - inner)).astype(BF)
        dv_ref[:, span] = dot_plain(probs.astype(BF), do).astype(BF)
        dk_ref[:, span] = dot_plain(grad_scores, q).astype(BF)
        grads.append(dot_first(k, grad_scores) * scale)
    dq_ref[...] = jnp.concatenate(grads, axis=0).T.astype(BF)


def attend_back(joined, logs, grad_mixed, segments, first, pairs):
    rows, length = segments.shape
    lane = 2 * HEAD_DIM
    all_pairs = joined.shape[1] // (3 * lane)

    def block(start):
        return pl.BlockSpec((length, lane), lambda r, h: (r, start + h))

    out = jax.ShapeDtypeStruct((rows * length, pairs * lane), BF)
    return pl.pallas_call(
        attend_back_kernel,
        grid=(rows, pairs),
        in_specs=[
            pl.BlockSpec((1, length, 1), lambda r, h: (r, 0, 0)),
            pl.BlockSpec((1, 1, length), lambda r, h: (r, 0, 0)),
            block(first),
            block(all_pairs + first),
            block(2 * all_pairs + first),
            pl.BlockSpec((1, 1, 2, length), lambda r, h: (r, h, 0, 0)),
            block(first),
        ],
        out_specs=[block(0), block(0), block(0)],
        out_shape=[out, out, out],
        scratch_shapes=[pltpu.VMEM((length, length), F32)],
        name="attend_back",
    )(segments[:, :, None], segments[:, None, :], joined, joined, joined, logs, grad_mixed)


ERF_TOP = (
    0.00022905065861350646,
    0.0034082910107109506,
    0.050955695062380861,
    0.18520832239976145,
    1.128379143519084,
)
ERF_LOW = (
    -1.1791602954361697e-7,
    0.000023547966471313185,
    0.0010179625278914885,
    0.014070470171167667,
    0.11098505178285362,
    0.49746925110067538,
    1.0,
)
ROOT_HALF = 0.7071067811865476
ERF_LIMIT = 3.832506856900711 / ROOT_HALF


def polynomial(coefficients, value, outer):
    last = len(coefficients) - 1
    scaled = [c * outer * 0.5 ** (last - i) for i, c in enumerate(coefficients)]
    total = jnp.full_like(value, scaled[0])
    for c in scaled[1:]:
        total = total * value + c
    return total


def gelu_both(values):
    kept = jnp.clip(values, -ERF_LIMIT, ERF_LIMIT)
    square = kept * kept
    top = kept * polynomial(ERF_TOP, square, 0.5 * ROOT_HALF)
    phi = 0.5 + top / polynomial(ERF_LOW, square, 1.0)
    density = jnp.exp2(values * values * -0.7213475204444817 - 1.3257480647361593)
    return values * phi, phi + values * density


def widen_kernel(tile, chunk):
    def body(where, x_ref, w_ref, shift_ref, act_ref, slope_ref, stay_ref, go_ref):
        first = where[3] == 0
        for start in range(0, x_ref.shape[0], tile):
            rows = slice(start, start + tile)
            hidden = dot_plain(x_ref[rows, :], w_ref[...]) + shift_ref[...]
            act, slope = gelu_both(hidden)
            act = act.astype(BF)
            act_ref[rows, :] = act
            slope_ref[rows, :] = slope.astype(BF)
            for i in range(act.shape[1] // (2 * chunk)):
                even = act[:, 2 * i * chunk : (2 * i + 1) * chunk]
                odd = act[:, (2 * i + 1) * chunk : (2 * i + 2) * chunk]
                span = slice(i * chunk, (i + 1) * chunk)
                stay_ref[rows, span] = jnp.where(first, even, odd)
                go_ref[rows, span] = jnp.where(first, odd, even)

    return body


def widen(wires, values, weight, shift):
    count, width = values.shape
    ff = weight.shape[1]
    chunk = ff // (wires.count * 2)
    cols = 512

    def block(size):
        return pl.BlockSpec((count, size), lambda j, p: (0, j))

    out = jax.ShapeDtypeStruct((count, ff), BF)
    part = jax.ShapeDtypeStruct((count, ff // 2), BF)
    return pl.pallas_call(
        widen_kernel(128, chunk),
        out_shape=[out, out, part, part],
        grid_spec=pltpu.PrefetchScalarGridSpec(
            num_scalar_prefetch=1,
            grid=(ff // cols,),
            in_specs=[
                pl.BlockSpec((count, width), lambda j, p: (0, 0)),
                pl.BlockSpec((width, cols), lambda j, p: (0, j)),
                pl.BlockSpec((1, cols), lambda j, p: (0, j)),
            ],
            out_specs=[block(cols), block(cols), block(cols // 2), block(cols // 2)],
        ),
        name="widen",
    )(wires.where, values, weight, shift[None])


def shards(
    tokens,
    segments,
    pad_mask,
    dest_shard,
    dest_slot,
    ln1_gain,
    ln1_bias,
    qkv_weight,
    qv_bias,
    out_weight,
    out_bias,
    ln2_gain,
    ln2_bias,
    fc1_weight,
    fc1_bias,
    fc2_weight,
    fc2_bias,
    learn_gain,
    learn_bias,
    maps_weight,
    maps_bias,
    out_grad,
):
    wires = Wires()
    seq = wires.seq
    rows_all, slots_half, width = tokens.shape
    ff = fc1_bias.shape[0] * wires.count * 2
    devices = wires.count * 2
    m = width // devices
    wide = ff // width
    rows_here = rows_all // 2
    row_len = slots_half * 2
    count_tok = rows_here * row_len
    records = rows_here * IMG_ROW
    capacity = out_grad.shape[1]

    vectors = [ln1_gain, ln1_bias, qv_bias[0], qv_bias[1], out_bias]
    vectors += [ln2_gain, ln2_bias, fc2_bias, fc1_bias]
    small = jnp.concatenate(vectors).reshape(8 + wide, m)
    n_small = small.shape[0]
    pad_cols = 256
    small_cols = jnp.pad(small.T, ((0, 0), (0, pad_cols - n_small)))

    def other_rows(value):
        return lax.dynamic_slice_in_dim(value, (1 - seq) * rows_here, rows_here, 0)

    def own_rows(value):
        return lax.dynamic_slice_in_dim(value, seq * rows_here, rows_here, 0)

    came = wires.swap(other_rows(tokens))
    mine = own_rows(tokens)
    first = jnp.where(seq == 0, mine, came)
    second = jnp.where(seq == 0, came, mine)
    inputs_low = jnp.concatenate([first, second], axis=1).reshape(count_tok, width)
    grad_came = wires.swap(out_grad)
    ga = Gather(wires, [qkv_weight, small_cols])
    gc = Gather(wires, [out_weight, fc1_weight])
    gd = Gather(wires, [fc2_weight])
    ga.step()
    gc.step(ga.flight)
    ga.step()
    gd.step(gc.flight)
    gc.step(ga.sends)
    ga.step(gc.sends)
    qkv_full, small_all = ga.result()
    small_full = small_all[:, :128].T[:n_small].astype(F32)
    norm1_gain, norm1_shift, q_shift, v_shift, out_shift, norm2_gain, norm2_shift, fc2_shift = [
        small_full[i] for i in range(8)
    ]
    fc1_shift = small_full[8:n_small].reshape(wide, devices, m).transpose(1, 0, 2).reshape(ff)
    seg = own_rows(segments)
    seg_flat = seg.reshape(count_tok)
    mask = (seg_flat >= 0).astype(F32)

    inputs = inputs_low.astype(F32)
    normed1, inverse1 = norm_stats(inputs)
    attn_in = (normed1 * norm1_gain + norm1_shift).astype(BF)
    qkv_out = dot_plain(attn_in, qkv_full)
    joined_shift = jnp.concatenate([q_shift, jnp.zeros_like(q_shift), v_shift])
    joined = (qkv_out + joined_shift).astype(BF)
    pairs = width // (4 * HEAD_DIM)
    mixed, logs = attend(joined, seg, 0, 2 * pairs)
    gc.step((mixed,))
    gd.step(gc.sends)
    out_full, fc1_full = gc.result()
    mixed = gate(mixed, gd.sends)
    resid1 = inputs + dot_plain(mixed, out_full) + out_shift
    normed2, inverse2 = norm_stats(resid1)
    mlp_in = (normed2 * norm2_gain + norm2_shift).astype(BF)
    activated_low, slope, act_stay, act_go = widen(wires, mlp_in, fc1_full, fc1_shift)
    gd.step((slope,))
    (fc2_full,) = gd.result()
    resid2 = resid1 + dot_plain(activated_low, fc2_full) + fc2_shift

    learn_scale = learn_gain.astype(F32)
    normed3, inverse3 = norm_stats(resid2)
    normed3_out = normed3 * learn_scale + learn_bias.astype(F32)
    map_weight = maps_weight.astype(F32)
    logits = dot_second(normed3_out, map_weight, HIGH) + maps_bias.astype(F32)
    sigmas = jax.nn.sigmoid(logits)
    map_vals = sigmas * mask[:, None]
    row_index = jnp.arange(count_tok, dtype=jnp.int32) // row_len
    owner = jnp.where(seg_flat >= 0, row_index * IMG_ROW + seg_flat, -1)
    select = (owner[:, None] == jnp.arange(records, dtype=jnp.int32)[None, :]).astype(F32)
    token_weights = (select[:, :, None] * map_vals[:, None, :]).reshape(count_tok, records * NTOK)
    sums = dot_first(token_weights, resid2, HIGH)
    counts = jnp.sum(select * mask[:, None], axis=0)
    divisor = jnp.maximum(counts, 1.0)
    positions = own_rows(dest_shard * capacity + dest_slot).reshape(records)
    routing = (
        (positions[None, :] == jnp.arange(2 * capacity, dtype=jnp.int32)[:, None])
        & (counts > 0.0)[None, :]
    ).astype(BF)
    pooled_here = (sums.reshape(records, NTOK * width) / divisor[:, None]).astype(BF)
    pooled_all = dot_plain(routing, pooled_here).astype(BF).reshape(2, capacity, NTOK * width)
    pooled_came = wires.swap(pick(pooled_all, 1 - seq, 0))
    pooled = (pick(pooled_all, seq, 0).astype(F32) + pooled_came.astype(F32)).astype(BF)
    pooled = pooled.reshape(1, capacity, NTOK, width)

    grad_own = out_grad.reshape(capacity, NTOK * width)
    grad_far = grad_came.reshape(capacity, NTOK * width)
    grad_pos = jnp.where(
        seq == 0,
        jnp.concatenate([grad_own, grad_far], axis=0),
        jnp.concatenate([grad_far, grad_own], axis=0),
    )
    grad_records = (dot_first(routing, grad_pos) / divisor[:, None]).astype(BF)
    grad_records = grad_records.reshape(records * NTOK, width).astype(F32)

    grad_resid2 = dot_plain(token_weights, grad_records, HIGH)
    grad_maps_all = dot_second(resid2, grad_records, HIGH).reshape(count_tok, records, NTOK)
    grad_map_vals = jnp.sum(grad_maps_all * select[:, :, None], axis=1)
    grad_logits = grad_map_vals * mask[:, None] * sigmas * (1.0 - sigmas)
    grad_maps_weight = dot_first(grad_logits, normed3_out, HIGH)
    grad_maps_bias = jnp.sum(grad_logits, axis=0)
    grad_normed3 = dot_plain(grad_logits, map_weight, HIGH)
    back_three, grad_learn_gain, grad_learn_bias = norm_backward(
        grad_normed3, normed3, inverse3, learn_scale
    )
    grad_resid2 = grad_resid2 + back_three
    grad_branch2 = grad_resid2.astype(BF)
    s_fc2 = Scatter(wires)
    grad_branch2 = gate(grad_branch2, s_fc2.add(activated_low, act_stay, act_go, grad_branch2))
    grad_fc2_shift = jnp.sum(grad_branch2.astype(F32), axis=0)
    grad_activ = dot_second(grad_branch2, fc2_full).astype(BF)
    grad_hidden = (grad_activ.astype(F32) * slope.astype(F32)).astype(BF)
    grad_hidden = gate(grad_hidden, s_fc2.inner())
    s_fc1 = Scatter(wires)
    grad_hidden = gate(grad_hidden, s_fc1.add(mlp_in, *halves(wires, mlp_in), grad_hidden)[:1])
    grad_fc1_shift = jnp.sum(grad_hidden.astype(F32), axis=0)
    grad_normed2 = dot_second(grad_hidden, fc1_full)
    back_two, grad_norm2_gain, grad_norm2_shift = norm_backward(
        grad_normed2, normed2, inverse2, norm2_gain
    )
    grad_resid1 = grad_resid2 + back_two
    grad_branch1 = grad_resid1.astype(BF)
    grad_branch1 = gate(grad_branch1, s_fc1.inner())
    s_a = Scatter(wires)
    sent = s_a.add(mixed, *halves(wires, mixed), grad_branch1)
    grad_out_shift = jnp.sum(grad_branch1.astype(F32), axis=0)
    grad_branch1 = gate(grad_branch1, sent)
    grad_mixed = dot_second(grad_branch1, out_full).astype(BF)
    grad_mixed = gate(grad_mixed, s_fc2.terms)
    dq_a, dk_a, dv_a = attend_back(joined, logs[:, :pairs], grad_mixed, seg, 0, pairs)
    grad_a = jnp.concatenate([dq_a, dk_a, dv_a], axis=1)
    attn_stay, attn_go = halves(wires, attn_in)
    sent = s_a.add(attn_in, attn_stay, attn_go, grad_a)
    grad_mixed = gate(grad_mixed, (sent, s_fc1.terms))
    dq_b, dk_b, dv_b = attend_back(joined, logs[:, pairs:], grad_mixed, seg, pairs, pairs)
    grad_b = jnp.concatenate([dq_b, dk_b, dv_b], axis=1)
    z_one = Outer(wires, [s_fc2, s_fc1], (grad_b,))
    grad_b = gate(grad_b, (s_a.inner(), z_one.sends))
    s_b = Scatter(wires)
    sent = s_b.add(attn_in, attn_stay, attn_go, grad_b)
    grad_a, grad_b = gate((grad_a, grad_b), sent)
    half = pairs * 2 * HEAD_DIM

    def normed1_part(grads, c):
        cuts = [slice(i * width + c * half, i * width + (c + 1) * half) for i in range(3)]
        return dot_second(grads, jnp.concatenate([qkv_full[:, cut] for cut in cuts], axis=1))

    grad_normed1 = normed1_part(grad_a, 0)
    grad_b = gate(grad_b, (s_b.inner(), grad_normed1))
    grad_normed1 = grad_normed1 + normed1_part(grad_b, 1)
    grad_normed1 = gate(grad_normed1, s_a.terms)
    back_one, grad_norm1_gain, grad_norm1_shift = norm_backward(
        grad_normed1, normed1, inverse1, norm1_gain
    )
    sum_q, sum_v = [
        jnp.concatenate(
            [jnp.sum(g[:, i * half : (i + 1) * half].astype(F32), axis=0) for g in (grad_a, grad_b)]
        )
        for i in (0, 2)
    ]
    little = jnp.concatenate(
        [
            jnp.stack(
                [
                    grad_norm1_gain,
                    grad_norm1_shift,
                    sum_q,
                    sum_v,
                    grad_out_shift,
                    grad_norm2_gain,
                    grad_norm2_shift,
                    grad_fc2_shift,
                    grad_learn_gain,
                    grad_learn_bias,
                    jnp.pad(grad_maps_bias, (0, width - NTOK)),
                ]
            ),
            grad_maps_weight,
            grad_fc1_shift.reshape(wide, width),
        ],
        axis=0,
    )
    little = sum_everywhere(wires, jnp.pad(little, ((0, -little.shape[0] % 8), (0, 0))))
    z_two = Outer(wires, [s_a, s_b], (back_one,))
    done_fc2, done_fc1 = z_one.result(z_two.sends)
    done_out, done_a, done_b = z_two.result()
    done_qkv = jnp.concatenate(
        [d[:, i * half : (i + 1) * half] for i in range(3) for d in (done_a, done_b)], axis=1
    )
    place = lax.axis_index("rows") * 2 + seq
    held = lax.dynamic_slice_in_dim(little[:8], place * m, m, 1)
    held_fc1 = lax.dynamic_slice_in_dim(
        little[11 + NTOK : 11 + NTOK + wide].reshape(ff), place * wide * m, wide * m, 0
    )
    grad_rows = (grad_resid1 + back_one).reshape(rows_here, row_len, width)
    grad_away = lax.dynamic_slice_in_dim(grad_rows, (1 - seq) * slots_half, slots_half, 1)
    grad_back = wires.swap(grad_away)
    grad_kept = lax.dynamic_slice_in_dim(grad_rows, seq * slots_half, slots_half, 1)
    grad_held = jnp.where(
        seq == 0,
        jnp.concatenate([grad_kept, grad_back], axis=0),
        jnp.concatenate([grad_back, grad_kept], axis=0),
    )
    return (
        pooled,
        grad_held,
        held[0],
        held[1],
        done_qkv,
        held[2:4],
        done_out,
        held[4],
        held[5],
        held[6],
        done_fc1,
        held_fc1,
        done_fc2,
        held[7],
        little[8],
        little[9],
        little[11 : 11 + NTOK],
        little[10, :NTOK],
    )


def solution(mesh):
    both = ("rows", "seq")
    in_specs = (
        P("rows", "seq", None),
        P("rows", None),
        P("rows", "seq"),
        P("rows", None),
        P("rows", None),
        P(both),
        P(both),
        P(both, None),
        P(None, both),
        P(both, None),
        P(both),
        P(both),
        P(both),
        P(both, None),
        P(both),
        P(both, None),
        P(both),
        P(),
        P(),
        P(),
        P(),
        P("rows", "seq", None, None),
    )
    out_specs = (
        P("rows", "seq", None, None),
        P("rows", "seq", None),
        P(both),
        P(both),
        P(both, None),
        P(None, both),
        P(both, None),
        P(both),
        P(both),
        P(both),
        P(both, None),
        P(both),
        P(both, None),
        P(both),
        P(),
        P(),
        P(),
        P(),
    )
    return jax.shard_map(shards, mesh=mesh, in_specs=in_specs, out_specs=out_specs, check_vma=False)
```

```python
import jax
import jax.numpy as jnp
from jax import lax
from jax.experimental import pallas as pl
from jax.experimental.pallas import tpu as pltpu
from jax.sharding import PartitionSpec as P

HEAD_DIM = 64
NTOK = 8
IMG_ROW = 10

EPSILON = 1e-06
NEGATIVE = -1e30
HIGH = lax.Precision.HIGH
BF = jnp.bfloat16
F32 = jnp.float32
SWAP = [(0, 1), (1, 0)]


def dot_plain(a, b, precision=None):
    return jnp.dot(a, b, precision=precision, preferred_element_type=F32)


def dot_first(a, b, precision=None):
    return lax.dot_general(
        a, b, (((0,), (0,)), ((), ())), precision=precision, preferred_element_type=F32
    )


def dot_second(a, b, precision=None):
    return lax.dot_general(
        a, b, (((1,), (1,)), ((), ())), precision=precision, preferred_element_type=F32
    )


def norm_stats(values):
    centred = values - jnp.mean(values, axis=-1, keepdims=True)
    inverse = lax.rsqrt(jnp.mean(centred * centred, axis=-1, keepdims=True) + EPSILON)
    return centred * inverse, inverse


def norm_backward(grad_out, normed, inverse, scale_vec):
    grad_unit = grad_out * scale_vec
    grad_in = inverse * (
        grad_unit
        - jnp.mean(grad_unit, axis=-1, keepdims=True)
        - normed * jnp.mean(grad_unit * normed, axis=-1, keepdims=True)
    )
    return (grad_in, jnp.sum(grad_out * normed, axis=0), jnp.sum(grad_out, axis=0))


def factors(count):
    if count == 16:
        return (4, 2, 2)
    if count == 128:
        return (4, 8, 4)
    return (count, 1, 1)


def rotation(dims, steps):
    pairs = []
    for a in range(dims[0]):
        for b in range(dims[1]):
            for c in range(dims[2]):
                up = [(d + s) % size for d, s, size in zip((a, b, c), steps, dims)]
                source = (a * dims[1] + b) * dims[2] + c
                pairs.append((source, (up[0] * dims[1] + up[1]) * dims[2] + up[2]))
    return pairs


def crossing(dims, flips):
    pairs = []
    for a in range(dims[0]):
        for b in range(dims[1]):
            for c in range(dims[2]):
                other = [d ^ f for d, f in zip((a, b, c), flips)]
                source = (a * dims[1] + b) * dims[2] + c
                pairs.append((source, (other[0] * dims[1] + other[1]) * dims[2] + other[2]))
    return pairs


class Wires:
    def __init__(self):
        self.count = lax.axis_size("rows")
        self.dims = factors(self.count)
        row = lax.axis_index("rows")
        self.digits = (
            row // (self.dims[1] * self.dims[2]),
            (row // self.dims[2]) % self.dims[1],
            row % self.dims[2],
        )
        self.seq = lax.axis_index("seq")
        self.where = jnp.stack([*self.digits, self.seq]).astype(jnp.int32)

        self.planes = [(y, x) for y in range(self.dims[1]) for x in range(self.dims[2])]

    def turn(self, value, z, y, x):
        return lax.ppermute(value, "rows", rotation(self.dims, (z, y, x)))

    def swap(self, value):
        return lax.ppermute(value, "seq", SWAP)


def gate(values, hold):
    return lax.optimization_barrier((values, hold))[0]


def stack_kernel(*refs):
    for i, ref in enumerate(refs[:-1]):
        refs[-1][i] = ref[...]


def regroup(weight):
    lane = 2 * HEAD_DIM
    pairs = weight.shape[1] // (3 * lane)

    def body(x_ref, out_ref):
        for pair in range(pairs):
            for i in range(3):
                at, source = (pair * 3 + i) * lane, (i * pairs + pair) * lane
                out_ref[:, at : at + lane] = x_ref[:, source : source + lane]

    out = jax.ShapeDtypeStruct(weight.shape, weight.dtype)
    return pl.pallas_call(body, out_shape=out, name="regroup")(weight)


def place_kernel(n_parts, dims, chunk, widths):
    k0, k1, k2 = dims
    planes = [(y, x) for y in range(k1) for x in range(k2)]

    def body(where, *refs):
        parts, outs = refs[:n_parts], refs[n_parts : n_parts + len(widths)]
        buf, sem_in, sem_out = refs[n_parts + len(widths) :]
        came = []
        for other in (0, 1):
            for i, (y, x) in enumerate(planes):
                part = parts[other * len(planes) + i]
                for z in range(k0):
                    spot = [
                        lax.rem(where[j] - r + dims[j], dims[j]) for j, r in enumerate((z, y, x))
                    ]
                    seat = lax.rem(where[3] + other, 2)
                    block = ((spot[0] * k1 + spot[1]) * k2 + spot[2]) * 2 + seat
                    rows = pl.ds(pl.multiple_of(block * chunk, chunk), chunk)
                    copy = pltpu.make_async_copy(part.at[z], buf.at[rows], sem_in.at[len(came)])
                    copy.start()
                    came.append((copy, rows))
        went = []
        for copy, rows in came:
            copy.wait()
            start = 0
            for out, width in zip(outs, widths):
                back = pltpu.make_async_copy(
                    buf.at[rows, pl.ds(start, width)], out.at[rows], sem_out.at[len(went)]
                )
                back.start()
                went.append(back)
                start += width
        for back in went:
            back.wait()

    return body


class Gather:
    def __init__(self, wires, shards):
        self.wires, self.shards = wires, shards
        self.widths = [s.shape[1] for s in shards]
        m, n = shards[0].shape[0], sum(self.widths)
        self.plain = bool(m % 32 or n % 128)
        self.flight, self.sends = (), ()
        self.stage = 0
        if not self.plain:
            self.shard = jnp.concatenate(shards, axis=1) if len(shards) > 1 else shards[0]

    def step(self, after=()):
        if self.plain:
            return
        wires, stage = self.wires, self.stage
        self.stage += 1
        if stage == 0:
            sends = [self.shard]
        elif stage == 1:
            tops = [self.shard, *self.flight]
            out = jax.ShapeDtypeStruct((len(tops), *self.shard.shape), self.shard.dtype)
            sends = [pl.pallas_call(stack_kernel, out_shape=out, name="stack")(*tops)]
        else:
            sends = [self.held, *self.flight]
        if after:
            sends = gate(sends, after)
        if stage == 0:
            self.flight = [wires.turn(sends[0], r, 0, 0) for r in range(1, wires.dims[0])]
        elif stage == 1:
            (self.held,) = sends
            self.flight = [wires.turn(sends[0], 0, y, x) for y, x in wires.planes[1:]]
        else:
            self.held = sends
            self.flight = [wires.swap(p) for p in sends]
        self.sends = sends

    def result(self):
        wires = self.wires
        if self.plain:
            both = ("rows", "seq")
            return [lax.all_gather(s, both, axis=0, tiled=True) for s in self.shards]
        m, n = self.shard.shape
        kind = self.shard.dtype
        parts = [*self.held, *self.flight]
        total = wires.count * 2
        return pl.pallas_call(
            place_kernel(len(parts), wires.dims, m, self.widths),
            out_shape=[jax.ShapeDtypeStruct((m * total, w), kind) for w in self.widths],
            grid_spec=pltpu.PrefetchScalarGridSpec(
                num_scalar_prefetch=1,
                grid=(1,),
                in_specs=[pl.BlockSpec(memory_space=pl.ANY)] * len(parts),
                out_specs=[pl.BlockSpec(memory_space=pl.ANY)] * len(self.widths),
                scratch_shapes=[
                    pltpu.VMEM((m * total, n), kind),
                    pltpu.SemaphoreType.DMA((total,)),
                    pltpu.SemaphoreType.DMA((len(self.widths) * total,)),
                ],
            ),
            name="place",
        )(wires.where, *parts)


def total_of(terms):
    wide = [t.astype(F32) for t in terms]
    return sum(wide[1:], wide[0])


def halves(wires, values):
    width = values.shape[1]
    m = width // (wires.count * 2)
    column = jnp.arange(width, dtype=jnp.int32)
    inside = column % (width // 2)
    seat = jnp.where(column < width // 2, wires.seq, 1 - wires.seq)
    source = (inside // m * 2 + seat) * m + inside % m
    chosen = (jnp.arange(width, dtype=jnp.int32)[:, None] == source[None, :]).astype(BF)
    both = dot_plain(values, chosen).astype(BF)
    return both[:, : width // 2], both[:, width // 2 :]


def inner_fold_kernel(dims, widths):
    n = len(widths)

    def body(where, *refs):
        kept, came, outs = refs[:n], refs[n : 2 * n], refs[2 * n :]
        early = pl.program_id(0) < dims[0] // 2

        def write(out, up, right):
            y = lax.rem(where[1] + up, dims[1])
            x = lax.rem(where[2] + right, dims[2])
            start = 0
            for a, b, width in zip(kept, came, widths):
                out[0, :, start : start + width] = a[0, y, x] + b[0, y, x]
                start += width

        write(outs[0], 0, 0)
        write(outs[1], 0, 1)
        write(outs[2], 1, 0)

        @pl.when(early)
        def _():
            write(outs[3], 1, 1)

        @pl.when(jnp.logical_not(early))
        def _():
            write(outs[4], 1, 1)

    return body


def relay_kernel(k0):
    def body(where, x_ref, y_ref, over_x, over_y, x_out, y_out):
        early = pl.program_id(0) < k0 // 2

        @pl.when(early)
        def _():
            x_out[...] = x_ref[...]
            y_out[...] = y_ref[...] + over_x[...]

        @pl.when(jnp.logical_not(early))
        def _():
            x_out[...] = x_ref[...] + over_y[...]
            y_out[...] = y_ref[...]

    return body


def outer_fold_kernel(dims, counts):
    n = sum(counts)

    def body(where, *refs):
        for step in range(dims[0]):
            spot = lax.rem(where[0] + step, dims[0])
            at, start = 0, 0
            for count in counts:
                width = refs[at].shape[2]
                total = total_of([r[spot] for r in refs[at : at + count]]).astype(BF)
                refs[n + step][:, start : start + width] = total
                at += count
                start += width

    return body


def prefetched(wires, body, grid, in_specs, out_specs, out_shape, args, name):
    return pl.pallas_call(
        body,
        out_shape=out_shape,
        grid_spec=pltpu.PrefetchScalarGridSpec(
            num_scalar_prefetch=1,
            grid=grid,
            in_specs=in_specs,
            out_specs=out_specs,
        ),
        name=name,
    )(wires.where, *args)


class Scatter:
    def __init__(self, wires):
        self.wires = wires
        self.widths, self.kept, self.got, self.whole, self.terms = [], [], [], [], ()

    def add(self, left, stay, go, right, hold=()):
        wires = self.wires
        width = right.shape[1]
        self.m = left.shape[1] // (wires.count * 2)
        square = wires.dims[1:] == (2, 2)
        self.plain = bool(self.m % 32 or width % 512) or not square
        self.widths.append(width)
        if self.plain:
            self.whole.append(dot_first(left, right))
            return ()
        shape = (*wires.dims, self.m, width)
        send = dot_first(go, right).astype(BF).reshape(shape)
        kept = dot_first(stay, gate(right, (send, hold))).astype(BF).reshape(shape)
        self.kept.append(kept)
        self.got.append(wires.swap(send))
        return send, kept

    def inner(self):
        if self.plain:
            return ()
        wires, m = self.wires, self.m
        k0, k1, k2 = wires.dims
        n = sum(self.widths)
        half = k0 // 2
        whole = pl.BlockSpec((1, m, n), lambda z, p: (z, 0, 0))
        self.low = pl.BlockSpec((1, m, n), lambda z, p: (jnp.minimum(z, half - 1), 0, 0))
        self.high = pl.BlockSpec((1, m, n), lambda z, p: (jnp.maximum(z - half, 0), 0, 0))
        self.shape = jax.ShapeDtypeStruct((k0, m, n), BF)
        part = jax.ShapeDtypeStruct((half, m, n), BF)
        outs = prefetched(
            wires,
            inner_fold_kernel(wires.dims, self.widths),
            (k0,),
            [pl.BlockSpec((1, k1, k2, m, w), lambda z, p: (z, 0, 0, 0, 0)) for w in self.widths] * 2,
            [whole, whole, whole, self.low, self.high],
            [self.shape, self.shape, self.shape, part, part],
            [*self.kept, *self.got],
            "fold_inner",
        )
        self.parts = [*outs[:3], wires.turn(outs[3], 0, 0, 1), wires.turn(outs[4], 0, 1, 0)]
        return outs

    def relay(self):
        if self.plain:
            return ()
        wires = self.wires
        own, *rest = self.parts
        whole = pl.BlockSpec((1, *self.shape.shape[1:]), lambda z, p: (z, 0, 0))
        outs = prefetched(
            wires,
            relay_kernel(wires.dims[0]),
            (wires.dims[0],),
            [whole, whole, self.low, self.high],
            [whole, whole],
            [self.shape, self.shape],
            rest,
            "relay",
        )
        self.terms = [own, wires.turn(outs[0], 0, 0, 1), wires.turn(outs[1], 0, 1, 0)]
        return outs


class Outer:
    def __init__(self, wires, groups, after=()):
        self.wires, self.groups = wires, groups
        self.plain = groups[0].plain
        if self.plain:
            self.sends = self.terms = ()
            return
        k0 = wires.dims[0]
        self.tall = max(g.m for g in groups)
        self.steps = 4
        self.rows = min(g.m for g in groups)
        terms = [g.terms for g in groups]
        if after:
            terms = gate(terms, after)
        specs, self.blocks = [], []
        for g in groups:
            width = sum(g.widths)
            if g.m == self.rows:
                self.blocks.append(width // self.steps)
                spec = pl.BlockSpec((k0, g.m, width // self.steps), lambda j, p: (0, 0, j))
            else:
                self.blocks.append(width)
                spec = pl.BlockSpec((k0, self.rows, width), lambda j, p: (0, j, 0))
            specs += [spec] * len(g.terms)
        n = sum(self.blocks)
        outs = prefetched(
            wires,
            outer_fold_kernel(wires.dims, [len(t) for t in terms]),
            (self.steps,),
            specs,
            [pl.BlockSpec((self.rows, n), lambda j, p: (0, j))] * k0,
            [jax.ShapeDtypeStruct((self.rows, n * self.steps), BF)] * k0,
            [t for group in terms for t in group],
            "fold_outer",
        )
        self.sends = outs
        self.terms = [outs[0]] + [wires.turn(outs[r], r, 0, 0) for r in range(1, k0)]

    def result(self, shapes, spots):
        if self.plain:
            both = ("rows", "seq")
            return [
                lax.psum_scatter(w, both, scatter_dimension=0, tiled=True)
                for g in self.groups
                for w in g.whole
            ]
        terms = self.terms
        moves, lane = [], 2 * HEAD_DIM
        for j in range(self.steps):
            start, product = j * sum(self.blocks), 0
            for g, block in zip(self.groups, self.blocks):
                for c in range(0, block, lane):
                    row, column, at = j * self.rows, c, product
                    if g.m == self.rows:
                        row, column = 0, j * block + c
                        while column >= g.widths[at - product]:
                            column -= g.widths[at - product]
                            at += 1
                    array, spot = spots[at]
                    moves.append((start + c, array, row, spot(column)))
                start += block
                product += len(g.widths)

        def body(*refs):
            for source, array, row, column in moves:
                piece = total_of([r[:, source : source + lane] for r in refs[: len(terms)]])
                refs[len(terms) + array][row : row + self.rows, column : column + lane] = piece

        return pl.pallas_call(
            body, out_shape=[jax.ShapeDtypeStruct(x, F32) for x in shapes], name="finish"
        )(*terms)


def pick(value, index, axis):
    return lax.dynamic_index_in_dim(value, index, axis, keepdims=False)


def sum_everywhere(wires, value):
    value = value + wires.swap(value)
    dims = wires.dims
    planes = [(0, y, x) for y, x in wires.planes]
    for flips in (planes, [(z, 0, 0) for z in range(dims[0])]):
        terms = [value] + [
            lax.ppermute(value, "rows", crossing(dims, flip)) for flip in flips[1:]
        ]
        while len(terms) > 1:
            terms = [a + b for a, b in zip(terms[::2], terms[1::2])]
        (value,) = terms
    return value


def head_of(joined_ref, h):
    starts = [(2 * i + h) * HEAD_DIM for i in range(3)]
    return [joined_ref[:, start : start + HEAD_DIM] for start in starts]


def attend_kernel(seg_col, seg_row, joined_ref, mixed_ref, log_ref, bias_ref):
    @pl.when(pl.program_id(1) == 0)
    def _():
        bias_ref[...] = jnp.where(seg_col[0] == seg_row[0], 0.0, NEGATIVE)

    scale = HEAD_DIM ** (-0.5)
    mixed = []
    for h in (0, 1):
        q, k, v = head_of(joined_ref, h)
        scores = dot_second(k, q * BF(scale)) + bias_ref[...]
        largest = jnp.max(scores, axis=0, keepdims=True)
        exponent = jnp.exp(scores - largest)
        summed = jnp.sum(exponent, axis=0, keepdims=True)
        probs = (exponent * (1.0 / summed)).astype(BF)
        mixed.append(dot_first(v, probs))
        log_ref[0, 0, h : h + 1, :] = largest + jnp.log(summed)
    mixed_ref[...] = jnp.concatenate(mixed, axis=0).T.astype(BF)


def attend(joined, segments, first, pairs):
    rows, length = segments.shape
    lane = 2 * HEAD_DIM

    return pl.pallas_call(
        attend_kernel,
        grid=(rows, pairs),
        in_specs=[
            pl.BlockSpec((1, length, 1), lambda r, h: (r, 0, 0)),
            pl.BlockSpec((1, 1, length), lambda r, h: (r, 0, 0)),
            pl.BlockSpec((length, 3 * lane), lambda r, h: (r, first + h)),
        ],
        out_specs=[
            pl.BlockSpec((length, lane), lambda r, h: (r, h)),
            pl.BlockSpec((1, 1, 2, length), lambda r, h: (r, h, 0, 0)),
        ],
        out_shape=[
            jax.ShapeDtypeStruct((rows * length, pairs * lane), BF),
            jax.ShapeDtypeStruct((rows, pairs, 2, length), F32),
        ],
        scratch_shapes=[pltpu.VMEM((length, length), F32)],
        name="attend",
    )(segments[:, :, None], segments[:, None, :], joined)


def attend_back_kernel(
    seg_col, seg_row, joined_ref, log_ref, do_ref, grad_ref, bias_ref
):
    @pl.when(pl.program_id(1) == 0)
    def _():
        bias_ref[...] = jnp.where(seg_col[0] == seg_row[0], 0.0, NEGATIVE)

    scale = HEAD_DIM ** (-0.5)
    grads = []
    for h in (0, 1):
        span = slice(h * HEAD_DIM, (h + 1) * HEAD_DIM)
        q, k, v = head_of(joined_ref, h)
        q = q * BF(scale)
        do = do_ref[:, span]
        scores = dot_second(k, q) + bias_ref[...]
        probs = jnp.exp(scores - log_ref[0, 0, h : h + 1, :])
        grad_probs = dot_second(v, do)
        inner = jnp.sum(probs * grad_probs, axis=0, keepdims=True)
        grad_scores = (probs * (grad_probs - inner)).astype(BF)
        lane = 2 * HEAD_DIM
        k_span = slice(lane + h * HEAD_DIM, lane + (h + 1) * HEAD_DIM)
        v_span = slice(2 * lane + h * HEAD_DIM, 2 * lane + (h + 1) * HEAD_DIM)
        grad_ref[:, v_span] = dot_plain(probs.astype(BF), do).astype(BF)
        grad_ref[:, k_span] = dot_plain(grad_scores, q).astype(BF)
        grads.append(dot_first(k, grad_scores) * scale)
    grad_ref[:, : 2 * HEAD_DIM] = jnp.concatenate(grads, axis=0).T.astype(BF)


def attend_back(joined, logs, grad_mixed, segments, first, pairs):
    rows, length = segments.shape
    lane = 2 * HEAD_DIM
    return pl.pallas_call(
        attend_back_kernel,
        grid=(rows, pairs),
        in_specs=[
            pl.BlockSpec((1, length, 1), lambda r, h: (r, 0, 0)),
            pl.BlockSpec((1, 1, length), lambda r, h: (r, 0, 0)),
            pl.BlockSpec((length, 3 * lane), lambda r, h: (r, first + h)),
            pl.BlockSpec((1, 1, 2, length), lambda r, h: (r, h, 0, 0)),
            pl.BlockSpec((length, lane), lambda r, h: (r, first + h)),
        ],
        out_specs=pl.BlockSpec((length, 3 * lane), lambda r, h: (r, h)),
        out_shape=jax.ShapeDtypeStruct((rows * length, 3 * pairs * lane), BF),
        scratch_shapes=[pltpu.VMEM((length, length), F32)],
        name="attend_back",
        cost_estimate=pl.CostEstimate(
            flops=3 * 40 * rows * pairs * length * length * HEAD_DIM,
            transcendentals=3 * 2 * rows * pairs * length * length,
            bytes_accessed=3 * 16 * rows * length * pairs * lane,
        ),
    )(segments[:, :, None], segments[:, None, :], joined, logs, grad_mixed)


ERF_TOP = (
    0.00022905065861350646,
    0.0034082910107109506,
    0.050955695062380861,
    0.18520832239976145,
    1.128379143519084,
)
ERF_LOW = (
    -1.1791602954361697e-7,
    0.000023547966471313185,
    0.0010179625278914885,
    0.014070470171167667,
    0.11098505178285362,
    0.49746925110067538,
    1.0,
)
ROOT_HALF = 0.7071067811865476
ERF_LIMIT = 3.832506856900711 / ROOT_HALF


def polynomial(coefficients, value, outer):
    last = len(coefficients) - 1
    scaled = [c * outer * 0.5 ** (last - i) for i, c in enumerate(coefficients)]
    total = jnp.full_like(value, scaled[0])
    for c in scaled[1:]:
        total = total * value + c
    return total


def gelu_both(values):
    kept = jnp.clip(values, -ERF_LIMIT, ERF_LIMIT)
    square = kept * kept
    top = kept * polynomial(ERF_TOP, square, 0.5 * ROOT_HALF)
    phi = 0.5 + top / polynomial(ERF_LOW, square, 1.0)
    density = jnp.exp2(values * values * -0.7213475204444817 - 1.3257480647361593)
    return values * phi, phi + values * density


def widen_kernel(tile, chunk):
    def body(where, x_ref, w_ref, shift_ref, act_ref, slope_ref, stay_ref, go_ref):
        first = where[3] == 0
        for start in range(0, x_ref.shape[0], tile):
            rows = slice(start, start + tile)
            hidden = dot_plain(x_ref[rows, :], w_ref[...]) + shift_ref[...]
            act, slope = gelu_both(hidden)
            act = act.astype(BF)
            act_ref[rows, :] = act
            slope_ref[rows, :] = slope.astype(BF)
            for i in range(act.shape[1] // (2 * chunk)):
                even = act[:, 2 * i * chunk : (2 * i + 1) * chunk]
                odd = act[:, (2 * i + 1) * chunk : (2 * i + 2) * chunk]
                span = slice(i * chunk, (i + 1) * chunk)
                stay_ref[rows, span] = jnp.where(first, even, odd)
                go_ref[rows, span] = jnp.where(first, odd, even)

    return body


def widen(wires, values, weight, shift):
    count, width = values.shape
    ff = weight.shape[1]
    chunk = ff // (wires.count * 2)
    cols = 512

    def block(size):
        return pl.BlockSpec((count, size), lambda j, p: (0, j))

    out = jax.ShapeDtypeStruct((count, ff), BF)
    part = jax.ShapeDtypeStruct((count, ff // 2), BF)
    return pl.pallas_call(
        widen_kernel(128, chunk),
        out_shape=[out, out, part, part],
        grid_spec=pltpu.PrefetchScalarGridSpec(
            num_scalar_prefetch=1,
            grid=(ff // cols,),
            in_specs=[
                pl.BlockSpec((count, width), lambda j, p: (0, 0)),
                pl.BlockSpec((width, cols), lambda j, p: (0, j)),
                pl.BlockSpec((1, cols), lambda j, p: (0, j)),
            ],
            out_specs=[block(cols), block(cols), block(cols // 2), block(cols // 2)],
        ),
        name="widen",
    )(wires.where, values, weight, shift[None])


def shards(
    tokens,
    segments,
    pad_mask,
    dest_shard,
    dest_slot,
    ln1_gain,
    ln1_bias,
    qkv_weight,
    qv_bias,
    out_weight,
    out_bias,
    ln2_gain,
    ln2_bias,
    fc1_weight,
    fc1_bias,
    fc2_weight,
    fc2_bias,
    learn_gain,
    learn_bias,
    maps_weight,
    maps_bias,
    out_grad,
):
    wires = Wires()
    seq = wires.seq
    rows_all, slots_half, width = tokens.shape
    ff = fc1_bias.shape[0] * wires.count * 2
    devices = wires.count * 2
    m = width // devices
    wide = ff // width
    rows_here = rows_all // 2
    row_len = slots_half * 2
    count_tok = rows_here * row_len
    records = rows_here * IMG_ROW
    capacity = out_grad.shape[1]

    vectors = [ln1_gain, ln1_bias, qv_bias[0], qv_bias[1], out_bias]
    vectors += [ln2_gain, ln2_bias, fc2_bias, fc1_bias]
    small = jnp.concatenate(vectors).reshape(8 + wide, m)
    n_small = small.shape[0]
    pad_cols = 128
    small_cols = jnp.pad(small.T, ((0, 0), (0, pad_cols - n_small)))

    def other_rows(value):
        return lax.dynamic_slice_in_dim(value, (1 - seq) * rows_here, rows_here, 0)

    def own_rows(value):
        return lax.dynamic_slice_in_dim(value, seq * rows_here, rows_here, 0)

    came = wires.swap(other_rows(tokens))
    mine = own_rows(tokens)
    first = jnp.where(seq == 0, mine, came)
    second = jnp.where(seq == 0, came, mine)
    inputs_low = jnp.concatenate([first, second], axis=1).reshape(count_tok, width)
    grad_came = wires.swap(out_grad)
    ga = Gather(wires, [regroup(qkv_weight), small_cols])
    gc = Gather(wires, [out_weight, fc1_weight])
    gd = Gather(wires, [fc2_weight])
    ga.step()
    gc.step(ga.flight)
    ga.step()
    gd.step(gc.flight)
    gc.step(ga.sends)
    ga.step(gc.sends)
    qkv_full, small_all = ga.result()
    small_full = small_all.T[:n_small].astype(F32)
    norm1_gain, norm1_shift, q_shift, v_shift, out_shift, norm2_gain, norm2_shift, fc2_shift = [
        small_full[i] for i in range(8)
    ]
    fc1_shift = small_full[8:n_small].reshape(wide, devices, m).transpose(1, 0, 2).reshape(ff)
    inputs_low = gate(inputs_low, grad_came)
    seg = own_rows(segments)
    seg_flat = seg.reshape(count_tok)
    mask = (seg_flat >= 0).astype(F32)

    inputs = inputs_low.astype(F32)
    normed1, inverse1 = norm_stats(inputs)
    attn_in = (normed1 * norm1_gain + norm1_shift).astype(BF)
    attn_in = gate(attn_in, gd.flight)
    qkv_out = dot_plain(attn_in, qkv_full)
    pairs = width // (4 * HEAD_DIM)
    joined_shift = jnp.stack([q_shift, jnp.zeros_like(q_shift), v_shift])
    joined_shift = joined_shift.reshape(3, 2 * pairs, 2 * HEAD_DIM).transpose(1, 0, 2).reshape(3 * width)
    joined = (qkv_out + joined_shift).astype(BF)
    mixed, logs = attend(joined, seg, 0, 2 * pairs)
    gc.step((mixed,))
    gd.step(gc.sends)
    out_full, fc1_full = gc.result()
    mixed = gate(mixed, gd.sends)
    resid1 = inputs + dot_plain(mixed, out_full) + out_shift
    normed2, inverse2 = norm_stats(resid1)
    mlp_in = (normed2 * norm2_gain + norm2_shift).astype(BF)
    activated_low, slope, act_stay, act_go = widen(wires, mlp_in, fc1_full, fc1_shift)
    gd.step((slope,))
    (fc2_full,) = gd.result()
    resid2 = resid1 + dot_plain(activated_low, fc2_full) + fc2_shift

    learn_scale = learn_gain.astype(F32)
    normed3, inverse3 = norm_stats(resid2)
    normed3_out = normed3 * learn_scale + learn_bias.astype(F32)
    map_weight = maps_weight.astype(F32)
    logits = dot_second(normed3_out, map_weight, HIGH) + maps_bias.astype(F32)
    sigmas = jax.nn.sigmoid(logits)
    map_vals = sigmas * mask[:, None]
    row_index = jnp.arange(count_tok, dtype=jnp.int32) // row_len
    owner = jnp.where(seg_flat >= 0, row_index * IMG_ROW + seg_flat, -1)
    select = (owner[:, None] == jnp.arange(records, dtype=jnp.int32)[None, :]).astype(F32)
    token_weights = (select[:, :, None] * map_vals[:, None, :]).reshape(count_tok, records * NTOK)
    sums = dot_first(token_weights, resid2, HIGH)
    counts = jnp.sum(select * mask[:, None], axis=0)
    divisor = jnp.maximum(counts, 1.0)
    positions = own_rows(dest_shard * capacity + dest_slot).reshape(records)
    routing = (
        (positions[None, :] == jnp.arange(2 * capacity, dtype=jnp.int32)[:, None])
        & (counts > 0.0)[None, :]
    ).astype(BF)
    pooled_here = (sums.reshape(records, NTOK * width) / divisor[:, None]).astype(BF)
    pooled_all = dot_plain(routing, pooled_here).astype(BF).reshape(2, capacity, NTOK * width)
    pooled_came = wires.swap(pick(pooled_all, 1 - seq, 0))
    pooled = (pick(pooled_all, seq, 0).astype(F32) + pooled_came.astype(F32)).astype(BF)
    pooled = pooled.reshape(1, capacity, NTOK, width)

    grad_own = out_grad.reshape(capacity, NTOK * width)
    grad_far = grad_came.reshape(capacity, NTOK * width)
    grad_pos = jnp.where(
        seq == 0,
        jnp.concatenate([grad_own, grad_far], axis=0),
        jnp.concatenate([grad_far, grad_own], axis=0),
    )
    grad_records = (dot_first(routing, grad_pos) / divisor[:, None]).astype(BF)
    grad_records = grad_records.reshape(records * NTOK, width).astype(F32)

    grad_resid2 = dot_plain(token_weights, grad_records, HIGH)
    grad_maps_all = dot_second(resid2, grad_records, HIGH).reshape(count_tok, records, NTOK)
    grad_map_vals = jnp.sum(grad_maps_all * select[:, :, None], axis=1)
    grad_logits = grad_map_vals * mask[:, None] * sigmas * (1.0 - sigmas)
    grad_maps_weight = dot_first(grad_logits, normed3_out, HIGH)
    grad_maps_bias = jnp.sum(grad_logits, axis=0)
    grad_normed3 = dot_plain(grad_logits, map_weight, HIGH)
    back_three, grad_learn_gain, grad_learn_bias = norm_backward(
        grad_normed3, normed3, inverse3, learn_scale
    )
    grad_resid2 = grad_resid2 + back_three
    grad_branch2 = grad_resid2.astype(BF)
    s_fc2 = Scatter(wires)
    grad_branch2 = gate(grad_branch2, s_fc2.add(activated_low, act_stay, act_go, grad_branch2))
    grad_fc2_shift = jnp.sum(grad_branch2.astype(F32), axis=0)
    grad_activ = dot_second(grad_branch2, fc2_full).astype(BF)
    grad_hidden = (grad_activ.astype(F32) * slope.astype(F32)).astype(BF)
    grad_hidden = gate(grad_hidden, (s_fc2.inner(), pooled, grad_fc2_shift, grad_maps_weight))
    s_fc1 = Scatter(wires)
    grad_hidden = gate(grad_hidden, s_fc1.add(mlp_in, *halves(wires, mlp_in), grad_hidden)[:1])
    grad_fc1_shift = jnp.sum(grad_hidden.astype(F32), axis=0)
    grad_hidden = gate(grad_hidden, s_fc2.relay())
    grad_normed2 = dot_second(grad_hidden, fc1_full)
    back_two, grad_norm2_gain, grad_norm2_shift = norm_backward(
        grad_normed2, normed2, inverse2, norm2_gain
    )
    grad_resid1 = grad_resid2 + back_two
    grad_branch1 = grad_resid1.astype(BF)
    grad_branch1 = gate(grad_branch1, (s_fc1.inner(), grad_fc1_shift))
    s_a = Scatter(wires)
    sent = s_a.add(mixed, *halves(wires, mixed), grad_branch1)
    grad_out_shift = jnp.sum(grad_branch1.astype(F32), axis=0)
    grad_branch1 = gate(grad_branch1, sent)
    grad_mixed = dot_second(grad_branch1, out_full).astype(BF)
    grad_mixed = gate(grad_mixed, (s_fc2.terms, grad_out_shift, s_fc1.relay()))
    grad_a = attend_back(joined, logs[:, :pairs], grad_mixed, seg, 0, pairs)
    attn_stay, attn_go = halves(wires, attn_in)
    sent = s_a.add(attn_in, attn_stay, attn_go, grad_a)
    grad_mixed = gate(grad_mixed, (sent, s_fc1.terms))
    grad_b = attend_back(joined, logs[:, pairs:], grad_mixed, seg, pairs, pairs)
    z_one = Outer(wires, [s_fc2, s_fc1], (grad_b,))
    grad_b = gate(grad_b, (s_a.inner(), z_one.sends))
    s_b = Scatter(wires)
    sent = s_b.add(attn_in, attn_stay, attn_go, grad_b)
    grad_a, grad_b = gate((grad_a, grad_b), sent)
    part = 6 * pairs * HEAD_DIM
    grad_a = gate(grad_a, s_a.relay())
    grad_normed1 = dot_second(grad_a, qkv_full[:, :part])
    grad_b = gate(grad_b, (s_b.inner(), grad_normed1, z_one.terms))
    grad_normed1 = grad_normed1 + dot_second(grad_b, qkv_full[:, part:])
    grad_normed1 = gate(grad_normed1, (s_a.terms, s_b.relay()))
    back_one, grad_norm1_gain, grad_norm1_shift = norm_backward(
        grad_normed1, normed1, inverse1, norm1_gain
    )
    sums_here = jnp.concatenate([jnp.sum(g.astype(F32), axis=0) for g in (grad_a, grad_b)])
    sums_here = sums_here.reshape(2 * pairs, 3, 2 * HEAD_DIM)
    sum_q, sum_v = sums_here[:, 0].reshape(width), sums_here[:, 2].reshape(width)
    little = jnp.concatenate(
        [
            jnp.stack(
                [
                    grad_norm1_gain,
                    grad_norm1_shift,
                    sum_q,
                    sum_v,
                    grad_out_shift,
                    grad_norm2_gain,
                    grad_norm2_shift,
                    grad_fc2_shift,
                    grad_learn_gain,
                    grad_learn_bias,
                    jnp.pad(grad_maps_bias, (0, width - NTOK)),
                ]
            ),
            grad_maps_weight,
            grad_fc1_shift.reshape(wide, width),
        ],
        axis=0,
    )
    z_two = Outer(wires, [s_a, s_b])
    little = jnp.pad(little, ((0, -little.shape[0] % 8), (0, 0)))
    little = sum_everywhere(wires, gate(little, z_two.sends))
    grad_rows = (grad_resid1 + back_one).reshape(rows_here, row_len, width)
    grad_away = lax.dynamic_slice_in_dim(grad_rows, (1 - seq) * slots_half, slots_half, 1)
    grad_back = wires.swap(grad_away)
    grad_kept = lax.dynamic_slice_in_dim(grad_rows, seq * slots_half, slots_half, 1)
    grad_held = jnp.where(
        seq == 0,
        jnp.concatenate([grad_kept, grad_back], axis=0),
        jnp.concatenate([grad_back, grad_kept], axis=0),
    )
    z_two.terms = gate(z_two.terms, grad_held)
    lane = 2 * HEAD_DIM

    def same(column):
        return column

    def spread(first):
        return lambda column: (
            column // lane % 3 * width + (first + column // (3 * lane)) * lane + column % lane
        )

    z_one.terms = gate(z_one.terms, z_two.sends)
    done_fc2, done_fc1 = z_one.result(
        [(wide * m, width), (m, ff)], [(0, same), (1, same)]
    )
    done_two = z_two.result(
        [(m, width), (m, 3 * width)], [(0, same), (1, spread(0)), (1, spread(pairs))]
    )
    done_out, done_qkv = done_two[0], done_two[1]
    if z_two.plain:
        done_qkv = jnp.concatenate(done_two[1:], axis=1).reshape(m, 2 * pairs, 3, lane)
        done_qkv = done_qkv.transpose(0, 2, 1, 3).reshape(m, 3 * width)
    place = lax.axis_index("rows") * 2 + seq
    held = lax.dynamic_slice_in_dim(little[:8], place * m, m, 1)
    held_fc1 = lax.dynamic_slice_in_dim(
        little[11 + NTOK : 11 + NTOK + wide].reshape(ff), place * wide * m, wide * m, 0
    )
    return (
        pooled,
        grad_held,
        held[0],
        held[1],
        done_qkv,
        held[2:4],
        done_out,
        held[4],
        held[5],
        held[6],
        done_fc1,
        held_fc1,
        done_fc2,
        held[7],
        little[8],
        little[9],
        little[11 : 11 + NTOK],
        little[10, :NTOK],
    )


def solution(mesh):
    both = ("rows", "seq")
    in_specs = (
        P("rows", "seq", None),
        P("rows", None),
        P("rows", "seq"),
        P("rows", None),
        P("rows", None),
        P(both),
        P(both),
        P(both, None),
        P(None, both),
        P(both, None),
        P(both),
        P(both),
        P(both),
        P(both, None),
        P(both),
        P(both, None),
        P(both),
        P(),
        P(),
        P(),
        P(),
        P("rows", "seq", None, None),
    )
    out_specs = (
        P("rows", "seq", None, None),
        P("rows", "seq", None),
        P(both),
        P(both),
        P(both, None),
        P(None, both),
        P(both, None),
        P(both),
        P(both),
        P(both),
        P(both, None),
        P(both),
        P(both, None),
        P(both),
        P(),
        P(),
        P(),
        P(),
    )
    return jax.shard_map(shards, mesh=mesh, in_specs=in_specs, out_specs=out_specs, check_vma=False)
```

```python
import jax
import jax.numpy as jnp
from jax import lax
from jax.experimental import pallas as pl
from jax.experimental.pallas import tpu as pltpu
from jax.sharding import PartitionSpec as P

HEAD_DIM = 64
NTOK = 8
IMG_ROW = 10

EPSILON = 1e-06
NEGATIVE = -1e30
HIGH = lax.Precision.HIGH
BF = jnp.bfloat16
F32 = jnp.float32
SWAP = [(0, 1), (1, 0)]


def dot_plain(a, b, precision=None):
    return jnp.dot(a, b, precision=precision, preferred_element_type=F32)


def dot_first(a, b, precision=None):
    return lax.dot_general(
        a, b, (((0,), (0,)), ((), ())), precision=precision, preferred_element_type=F32
    )


def dot_second(a, b, precision=None):
    return lax.dot_general(
        a, b, (((1,), (1,)), ((), ())), precision=precision, preferred_element_type=F32
    )


def norm_stats(values):
    centred = values - jnp.mean(values, axis=-1, keepdims=True)
    inverse = lax.rsqrt(jnp.mean(centred * centred, axis=-1, keepdims=True) + EPSILON)
    return centred * inverse, inverse


def norm_backward(grad_out, normed, inverse, scale_vec):
    grad_unit = grad_out * scale_vec
    grad_in = inverse * (
        grad_unit
        - jnp.mean(grad_unit, axis=-1, keepdims=True)
        - normed * jnp.mean(grad_unit * normed, axis=-1, keepdims=True)
    )
    return (grad_in, jnp.sum(grad_out * normed, axis=0), jnp.sum(grad_out, axis=0))


def factors(count):
    if count == 16:
        return (4, 2, 2)
    if count == 128:
        return (4, 8, 4)
    return (count, 1, 1)


def rotation(dims, steps):
    pairs = []
    for a in range(dims[0]):
        for b in range(dims[1]):
            for c in range(dims[2]):
                up = [(d + s) % size for d, s, size in zip((a, b, c), steps, dims)]
                source = (a * dims[1] + b) * dims[2] + c
                pairs.append((source, (up[0] * dims[1] + up[1]) * dims[2] + up[2]))
    return pairs


def crossing(dims, flips):
    pairs = []
    for a in range(dims[0]):
        for b in range(dims[1]):
            for c in range(dims[2]):
                other = [d ^ f for d, f in zip((a, b, c), flips)]
                source = (a * dims[1] + b) * dims[2] + c
                pairs.append((source, (other[0] * dims[1] + other[1]) * dims[2] + other[2]))
    return pairs


class Wires:
    def __init__(self):
        self.count = lax.axis_size("rows")
        self.dims = factors(self.count)
        row = lax.axis_index("rows")
        self.digits = (
            row // (self.dims[1] * self.dims[2]),
            (row // self.dims[2]) % self.dims[1],
            row % self.dims[2],
        )
        self.seq = lax.axis_index("seq")
        self.where = jnp.stack([*self.digits, self.seq]).astype(jnp.int32)

        self.planes = [(y, x) for y in range(self.dims[1]) for x in range(self.dims[2])]

    def turn(self, value, z, y, x):
        return lax.ppermute(value, "rows", rotation(self.dims, (z, y, x)))

    def swap(self, value):
        return lax.ppermute(value, "seq", SWAP)


def gate(values, hold):
    return lax.optimization_barrier((values, hold))[0]


def stack_kernel(*refs):
    for i, ref in enumerate(refs[:-1]):
        refs[-1][i] = ref[...]


def regroup(weight):
    lane = 2 * HEAD_DIM
    pairs = weight.shape[1] // (3 * lane)

    def body(x_ref, out_ref):
        for pair in range(pairs):
            for i in range(3):
                at, source = (pair * 3 + i) * lane, (i * pairs + pair) * lane
                out_ref[:, at : at + lane] = x_ref[:, source : source + lane]

    out = jax.ShapeDtypeStruct(weight.shape, weight.dtype)
    return pl.pallas_call(body, out_shape=out, name="regroup")(weight)


def place_kernel(n_parts, dims, chunk, widths):
    k0, k1, k2 = dims
    planes = [(y, x) for y in range(k1) for x in range(k2)]

    def body(where, *refs):
        parts, outs = refs[:n_parts], refs[n_parts : n_parts + len(widths)]
        buf, sem_in, sem_out = refs[n_parts + len(widths) :]
        came = []
        for other in (0, 1):
            for i, (y, x) in enumerate(planes):
                part = parts[other * len(planes) + i]
                for z in range(k0):
                    spot = [
                        lax.rem(where[j] - r + dims[j], dims[j]) for j, r in enumerate((z, y, x))
                    ]
                    seat = lax.rem(where[3] + other, 2)
                    block = ((spot[0] * k1 + spot[1]) * k2 + spot[2]) * 2 + seat
                    rows = pl.ds(pl.multiple_of(block * chunk, chunk), chunk)
                    copy = pltpu.make_async_copy(part.at[z], buf.at[rows], sem_in.at[len(came)])
                    copy.start()
                    came.append((copy, rows))
        went = []
        for copy, rows in came:
            copy.wait()
            start = 0
            for out, width in zip(outs, widths):
                back = pltpu.make_async_copy(
                    buf.at[rows, pl.ds(start, width)], out.at[rows], sem_out.at[len(went)]
                )
                back.start()
                went.append(back)
                start += width
        for back in went:
            back.wait()

    return body


class Gather:
    def __init__(self, wires, shards):
        self.wires, self.shards = wires, shards
        self.widths = [s.shape[1] for s in shards]
        m, n = shards[0].shape[0], sum(self.widths)
        self.plain = bool(m % 32 or n % 128)
        self.flight, self.sends = (), ()
        self.stage = 0
        if not self.plain:
            self.shard = jnp.concatenate(shards, axis=1) if len(shards) > 1 else shards[0]

    def step(self, after=()):
        if self.plain:
            return
        wires, stage = self.wires, self.stage
        self.stage += 1
        if stage == 0:
            sends = [self.shard]
        elif stage == 1:
            tops = [self.shard, *self.flight]
            out = jax.ShapeDtypeStruct((len(tops), *self.shard.shape), self.shard.dtype)
            sends = [pl.pallas_call(stack_kernel, out_shape=out, name="stack")(*tops)]
        else:
            sends = [self.held, *self.flight]
        if after:
            sends = gate(sends, after)
        if stage == 0:
            self.flight = [wires.turn(sends[0], r, 0, 0) for r in range(1, wires.dims[0])]
        elif stage == 1:
            (self.held,) = sends
            self.flight = [wires.turn(sends[0], 0, y, x) for y, x in wires.planes[1:]]
        else:
            self.held = sends
            self.flight = [wires.swap(p) for p in sends]
        self.sends = sends

    def result(self):
        wires = self.wires
        if self.plain:
            both = ("rows", "seq")
            return [lax.all_gather(s, both, axis=0, tiled=True) for s in self.shards]
        m, n = self.shard.shape
        kind = self.shard.dtype
        parts = [*self.held, *self.flight]
        total = wires.count * 2
        return pl.pallas_call(
            place_kernel(len(parts), wires.dims, m, self.widths),
            out_shape=[jax.ShapeDtypeStruct((m * total, w), kind) for w in self.widths],
            grid_spec=pltpu.PrefetchScalarGridSpec(
                num_scalar_prefetch=1,
                grid=(1,),
                in_specs=[pl.BlockSpec(memory_space=pl.ANY)] * len(parts),
                out_specs=[pl.BlockSpec(memory_space=pl.ANY)] * len(self.widths),
                scratch_shapes=[
                    pltpu.VMEM((m * total, n), kind),
                    pltpu.SemaphoreType.DMA((total,)),
                    pltpu.SemaphoreType.DMA((len(self.widths) * total,)),
                ],
            ),
            name="place",
        )(wires.where, *parts)


def total_of(terms):
    wide = [t.astype(F32) for t in terms]
    return sum(wide[1:], wide[0])


def halves(wires, values):
    width = values.shape[1]
    m = width // (wires.count * 2)
    column = jnp.arange(width, dtype=jnp.int32)
    inside = column % (width // 2)
    seat = jnp.where(column < width // 2, wires.seq, 1 - wires.seq)
    source = (inside // m * 2 + seat) * m + inside % m
    chosen = (jnp.arange(width, dtype=jnp.int32)[:, None] == source[None, :]).astype(BF)
    both = dot_plain(values, chosen).astype(BF)
    return both[:, : width // 2], both[:, width // 2 :]


def inner_fold_kernel(dims, widths):
    n = len(widths)

    def body(where, *refs):
        kept, came, outs = refs[:n], refs[n : 2 * n], refs[2 * n :]
        early = pl.program_id(0) < dims[0] // 2

        def write(out, up, right):
            y = lax.rem(where[1] + up, dims[1])
            x = lax.rem(where[2] + right, dims[2])
            start = 0
            for a, b, width in zip(kept, came, widths):
                out[0, :, start : start + width] = a[0, y, x] + b[0, y, x]
                start += width

        write(outs[0], 0, 0)
        write(outs[1], 0, 1)
        write(outs[2], 1, 0)

        @pl.when(early)
        def _():
            write(outs[3], 1, 1)

        @pl.when(jnp.logical_not(early))
        def _():
            write(outs[4], 1, 1)

    return body


def relay_kernel(k0):
    def body(where, x_ref, y_ref, over_x, over_y, x_out, y_out):
        early = pl.program_id(0) < k0 // 2

        @pl.when(early)
        def _():
            x_out[...] = x_ref[...]
            y_out[...] = y_ref[...] + over_x[...]

        @pl.when(jnp.logical_not(early))
        def _():
            x_out[...] = x_ref[...] + over_y[...]
            y_out[...] = y_ref[...]

    return body


def outer_fold_kernel(dims, counts):
    n = sum(counts)

    def body(where, *refs):
        for step in range(dims[0]):
            spot = lax.rem(where[0] + step, dims[0])
            at, start = 0, 0
            for count in counts:
                width = refs[at].shape[2]
                total = total_of([r[spot] for r in refs[at : at + count]]).astype(BF)
                refs[n + step][:, start : start + width] = total
                at += count
                start += width

    return body


def prefetched(wires, body, grid, in_specs, out_specs, out_shape, args, name):
    return pl.pallas_call(
        body,
        out_shape=out_shape,
        grid_spec=pltpu.PrefetchScalarGridSpec(
            num_scalar_prefetch=1,
            grid=grid,
            in_specs=in_specs,
            out_specs=out_specs,
        ),
        name=name,
    )(wires.where, *args)


class Scatter:
    def __init__(self, wires):
        self.wires = wires
        self.widths, self.kept, self.got, self.whole, self.terms = [], [], [], [], ()

    def add(self, left, stay, go, right, hold=()):
        wires = self.wires
        width = right.shape[1]
        self.m = left.shape[1] // (wires.count * 2)
        square = wires.dims[1:] == (2, 2)
        self.plain = bool(self.m % 32 or width % 512) or not square
        self.widths.append(width)
        if self.plain:
            self.whole.append(dot_first(left, right))
            return ()
        shape = (*wires.dims, self.m, width)
        send = dot_first(go, right).astype(BF).reshape(shape)
        kept = dot_first(stay, gate(right, (send, hold))).astype(BF).reshape(shape)
        self.kept.append(kept)
        self.got.append(wires.swap(send))
        return send, kept

    def inner(self):
        if self.plain:
            return ()
        wires, m = self.wires, self.m
        k0, k1, k2 = wires.dims
        n = sum(self.widths)
        half = k0 // 2
        whole = pl.BlockSpec((1, m, n), lambda z, p: (z, 0, 0))
        self.low = pl.BlockSpec((1, m, n), lambda z, p: (jnp.minimum(z, half - 1), 0, 0))
        self.high = pl.BlockSpec((1, m, n), lambda z, p: (jnp.maximum(z - half, 0), 0, 0))
        self.shape = jax.ShapeDtypeStruct((k0, m, n), BF)
        part = jax.ShapeDtypeStruct((half, m, n), BF)
        outs = prefetched(
            wires,
            inner_fold_kernel(wires.dims, self.widths),
            (k0,),
            [pl.BlockSpec((1, k1, k2, m, w), lambda z, p: (z, 0, 0, 0, 0)) for w in self.widths] * 2,
            [whole, whole, whole, self.low, self.high],
            [self.shape, self.shape, self.shape, part, part],
            [*self.kept, *self.got],
            "fold_inner",
        )
        self.parts = [*outs[:3], wires.turn(outs[3], 0, 0, 1), wires.turn(outs[4], 0, 1, 0)]
        return outs

    def relay(self):
        if self.plain:
            return ()
        wires = self.wires
        own, *rest = self.parts
        whole = pl.BlockSpec((1, *self.shape.shape[1:]), lambda z, p: (z, 0, 0))
        outs = prefetched(
            wires,
            relay_kernel(wires.dims[0]),
            (wires.dims[0],),
            [whole, whole, self.low, self.high],
            [whole, whole],
            [self.shape, self.shape],
            rest,
            "relay",
        )
        self.terms = [own, wires.turn(outs[0], 0, 0, 1), wires.turn(outs[1], 0, 1, 0)]
        return outs


class Outer:
    def __init__(self, wires, groups, after=()):
        self.wires, self.groups = wires, groups
        self.plain = groups[0].plain
        if self.plain:
            self.sends = self.terms = ()
            return
        k0 = wires.dims[0]
        self.tall = max(g.m for g in groups)
        self.steps = 4
        self.rows = min(g.m for g in groups)
        terms = [g.terms for g in groups]
        if after:
            terms = gate(terms, after)
        specs, self.blocks = [], []
        for g in groups:
            width = sum(g.widths)
            if g.m == self.rows:
                self.blocks.append(width // self.steps)
                spec = pl.BlockSpec((k0, g.m, width // self.steps), lambda j, p: (0, 0, j))
            else:
                self.blocks.append(width)
                spec = pl.BlockSpec((k0, self.rows, width), lambda j, p: (0, j, 0))
            specs += [spec] * len(g.terms)
        n = sum(self.blocks)
        outs = prefetched(
            wires,
            outer_fold_kernel(wires.dims, [len(t) for t in terms]),
            (self.steps,),
            specs,
            [pl.BlockSpec((self.rows, n), lambda j, p: (0, j))] * k0,
            [jax.ShapeDtypeStruct((self.rows, n * self.steps), BF)] * k0,
            [t for group in terms for t in group],
            "fold_outer",
        )
        self.sends = outs
        self.terms = [outs[0]] + [wires.turn(outs[r], r, 0, 0) for r in range(1, k0)]

    def result(self, shapes, spots):
        if self.plain:
            both = ("rows", "seq")
            return [
                lax.psum_scatter(w, both, scatter_dimension=0, tiled=True)
                for g in self.groups
                for w in g.whole
            ]
        terms = self.terms
        moves, lane = [], 2 * HEAD_DIM
        for j in range(self.steps):
            start, product = j * sum(self.blocks), 0
            for g, block in zip(self.groups, self.blocks):
                for c in range(0, block, lane):
                    row, column, at = j * self.rows, c, product
                    if g.m == self.rows:
                        row, column = 0, j * block + c
                        while column >= g.widths[at - product]:
                            column -= g.widths[at - product]
                            at += 1
                    array, spot = spots[at]
                    moves.append((start + c, array, row, spot(column)))
                start += block
                product += len(g.widths)

        def body(*refs):
            for source, array, row, column in moves:
                piece = total_of([r[:, source : source + lane] for r in refs[: len(terms)]])
                refs[len(terms) + array][row : row + self.rows, column : column + lane] = piece

        return pl.pallas_call(
            body, out_shape=[jax.ShapeDtypeStruct(x, F32) for x in shapes], name="finish"
        )(*terms)


def pick(value, index, axis):
    return lax.dynamic_index_in_dim(value, index, axis, keepdims=False)


def sum_everywhere(wires, value, hold):
    value = value + wires.swap(value)
    dims = wires.dims
    planes = [(0, y, x) for y, x in wires.planes]
    for flips in (planes, [(z, 0, 0) for z in range(dims[0])]):
        if flips is not planes:
            value = gate(value, hold)
        terms = [value] + [
            lax.ppermute(value, "rows", crossing(dims, flip)) for flip in flips[1:]
        ]
        while len(terms) > 1:
            terms = [a + b for a, b in zip(terms[::2], terms[1::2])]
        (value,) = terms
    return value


def head_of(joined_ref, h):
    starts = [(2 * i + h) * HEAD_DIM for i in range(3)]
    return [joined_ref[:, start : start + HEAD_DIM] for start in starts]


def attend_kernel(seg_col, seg_row, joined_ref, mixed_ref, log_ref, bias_ref):
    @pl.when(pl.program_id(1) == 0)
    def _():
        bias_ref[...] = jnp.where(seg_col[0] == seg_row[0], 0.0, NEGATIVE)

    scale = HEAD_DIM ** (-0.5)
    mixed = []
    for h in (0, 1):
        q, k, v = head_of(joined_ref, h)
        scores = dot_second(k, q * BF(scale)) + bias_ref[...]
        largest = jnp.max(scores, axis=0, keepdims=True)
        exponent = jnp.exp(scores - largest)
        summed = jnp.sum(exponent, axis=0, keepdims=True)
        probs = (exponent * (1.0 / summed)).astype(BF)
        mixed.append(dot_first(v, probs))
        log_ref[0, 0, h : h + 1, :] = largest + jnp.log(summed)
    mixed_ref[...] = jnp.concatenate(mixed, axis=0).T.astype(BF)


def attend(joined, segments, first, pairs):
    rows, length = segments.shape
    lane = 2 * HEAD_DIM

    return pl.pallas_call(
        attend_kernel,
        grid=(rows, pairs),
        in_specs=[
            pl.BlockSpec((1, length, 1), lambda r, h: (r, 0, 0)),
            pl.BlockSpec((1, 1, length), lambda r, h: (r, 0, 0)),
            pl.BlockSpec((length, 3 * lane), lambda r, h: (r, first + h)),
        ],
        out_specs=[
            pl.BlockSpec((length, lane), lambda r, h: (r, h)),
            pl.BlockSpec((1, 1, 2, length), lambda r, h: (r, h, 0, 0)),
        ],
        out_shape=[
            jax.ShapeDtypeStruct((rows * length, pairs * lane), BF),
            jax.ShapeDtypeStruct((rows, pairs, 2, length), F32),
        ],
        scratch_shapes=[pltpu.VMEM((length, length), F32)],
        name="attend",
    )(segments[:, :, None], segments[:, None, :], joined)


def attend_back_kernel(
    seg_col, seg_row, joined_ref, log_ref, do_ref, grad_ref, bias_ref
):
    @pl.when(pl.program_id(1) == 0)
    def _():
        bias_ref[...] = jnp.where(seg_col[0] == seg_row[0], 0.0, NEGATIVE)

    scale = HEAD_DIM ** (-0.5)
    grads = []
    for h in (0, 1):
        span = slice(h * HEAD_DIM, (h + 1) * HEAD_DIM)
        q, k, v = head_of(joined_ref, h)
        q = q * BF(scale)
        do = do_ref[:, span]
        scores = dot_second(k, q) + bias_ref[...]
        probs = jnp.exp(scores - log_ref[0, 0, h : h + 1, :])
        grad_probs = dot_second(v, do)
        inner = jnp.sum(probs * grad_probs, axis=0, keepdims=True)
        grad_scores = (probs * (grad_probs - inner)).astype(BF)
        lane = 2 * HEAD_DIM
        k_span = slice(lane + h * HEAD_DIM, lane + (h + 1) * HEAD_DIM)
        v_span = slice(2 * lane + h * HEAD_DIM, 2 * lane + (h + 1) * HEAD_DIM)
        grad_ref[:, v_span] = dot_plain(probs.astype(BF), do).astype(BF)
        grad_ref[:, k_span] = dot_plain(grad_scores, q).astype(BF)
        grads.append(dot_first(k, grad_scores) * scale)
    grad_ref[:, : 2 * HEAD_DIM] = jnp.concatenate(grads, axis=0).T.astype(BF)


def attend_back(joined, logs, grad_mixed, segments, first, pairs):
    rows, length = segments.shape
    lane = 2 * HEAD_DIM
    return pl.pallas_call(
        attend_back_kernel,
        grid=(rows, pairs),
        in_specs=[
            pl.BlockSpec((1, length, 1), lambda r, h: (r, 0, 0)),
            pl.BlockSpec((1, 1, length), lambda r, h: (r, 0, 0)),
            pl.BlockSpec((length, 3 * lane), lambda r, h: (r, first + h)),
            pl.BlockSpec((1, 1, 2, length), lambda r, h: (r, h, 0, 0)),
            pl.BlockSpec((length, lane), lambda r, h: (r, first + h)),
        ],
        out_specs=pl.BlockSpec((length, 3 * lane), lambda r, h: (r, h)),
        out_shape=jax.ShapeDtypeStruct((rows * length, 3 * pairs * lane), BF),
        scratch_shapes=[pltpu.VMEM((length, length), F32)],
        name="attend_back",
        cost_estimate=pl.CostEstimate(
            flops=3 * 40 * rows * pairs * length * length * HEAD_DIM,
            transcendentals=3 * 2 * rows * pairs * length * length,
            bytes_accessed=3 * 16 * rows * length * pairs * lane,
        ),
    )(segments[:, :, None], segments[:, None, :], joined, logs, grad_mixed)


ERF_TOP = (
    0.00022905065861350646,
    0.0034082910107109506,
    0.050955695062380861,
    0.18520832239976145,
    1.128379143519084,
)
ERF_LOW = (
    -1.1791602954361697e-7,
    0.000023547966471313185,
    0.0010179625278914885,
    0.014070470171167667,
    0.11098505178285362,
    0.49746925110067538,
    1.0,
)
ROOT_HALF = 0.7071067811865476
ERF_LIMIT = 3.832506856900711 / ROOT_HALF


def polynomial(coefficients, value, outer):
    last = len(coefficients) - 1
    scaled = [c * outer * 0.5 ** (last - i) for i, c in enumerate(coefficients)]
    total = jnp.full_like(value, scaled[0])
    for c in scaled[1:]:
        total = total * value + c
    return total


def gelu_both(values):
    kept = jnp.clip(values, -ERF_LIMIT, ERF_LIMIT)
    square = kept * kept
    top = kept * polynomial(ERF_TOP, square, 0.5 * ROOT_HALF)
    phi = 0.5 + top / polynomial(ERF_LOW, square, 1.0)
    density = jnp.exp2(values * values * -0.7213475204444817 - 1.3257480647361593)
    return values * phi, phi + values * density


def widen_kernel(tile, chunk):
    def body(where, x_ref, w_ref, shift_ref, act_ref, slope_ref, stay_ref, go_ref):
        first = where[3] == 0
        for start in range(0, x_ref.shape[0], tile):
            rows = slice(start, start + tile)
            hidden = dot_plain(x_ref[rows, :], w_ref[...]) + shift_ref[...]
            act, slope = gelu_both(hidden)
            act = act.astype(BF)
            act_ref[rows, :] = act
            slope_ref[rows, :] = slope.astype(BF)
            for i in range(act.shape[1] // (2 * chunk)):
                even = act[:, 2 * i * chunk : (2 * i + 1) * chunk]
                odd = act[:, (2 * i + 1) * chunk : (2 * i + 2) * chunk]
                span = slice(i * chunk, (i + 1) * chunk)
                stay_ref[rows, span] = jnp.where(first, even, odd)
                go_ref[rows, span] = jnp.where(first, odd, even)

    return body


def widen(wires, values, weight, shift):
    count, width = values.shape
    ff = weight.shape[1]
    chunk = ff // (wires.count * 2)
    cols = 512

    def block(size):
        return pl.BlockSpec((count, size), lambda j, p: (0, j))

    out = jax.ShapeDtypeStruct((count, ff), BF)
    part = jax.ShapeDtypeStruct((count, ff // 2), BF)
    return pl.pallas_call(
        widen_kernel(128, chunk),
        out_shape=[out, out, part, part],
        grid_spec=pltpu.PrefetchScalarGridSpec(
            num_scalar_prefetch=1,
            grid=(ff // cols,),
            in_specs=[
                pl.BlockSpec((count, width), lambda j, p: (0, 0)),
                pl.BlockSpec((width, cols), lambda j, p: (0, j)),
                pl.BlockSpec((1, cols), lambda j, p: (0, j)),
            ],
            out_specs=[block(cols), block(cols), block(cols // 2), block(cols // 2)],
        ),
        name="widen",
    )(wires.where, values, weight, shift[None])


def shards(
    tokens,
    segments,
    pad_mask,
    dest_shard,
    dest_slot,
    ln1_gain,
    ln1_bias,
    qkv_weight,
    qv_bias,
    out_weight,
    out_bias,
    ln2_gain,
    ln2_bias,
    fc1_weight,
    fc1_bias,
    fc2_weight,
    fc2_bias,
    learn_gain,
    learn_bias,
    maps_weight,
    maps_bias,
    out_grad,
):
    wires = Wires()
    seq = wires.seq
    rows_all, slots_half, width = tokens.shape
    ff = fc1_bias.shape[0] * wires.count * 2
    devices = wires.count * 2
    m = width // devices
    wide = ff // width
    rows_here = rows_all // 2
    row_len = slots_half * 2
    count_tok = rows_here * row_len
    records = rows_here * IMG_ROW
    capacity = out_grad.shape[1]

    vectors = [ln1_gain, ln1_bias, qv_bias[0], qv_bias[1], out_bias]
    vectors += [ln2_gain, ln2_bias, fc2_bias, fc1_bias]
    small = jnp.concatenate(vectors).reshape(8 + wide, m)
    n_small = small.shape[0]
    pad_cols = 128
    small_cols = jnp.pad(small.T, ((0, 0), (0, pad_cols - n_small)))

    def other_rows(value):
        return lax.dynamic_slice_in_dim(value, (1 - seq) * rows_here, rows_here, 0)

    def own_rows(value):
        return lax.dynamic_slice_in_dim(value, seq * rows_here, rows_here, 0)

    came = wires.swap(other_rows(tokens))
    mine = own_rows(tokens)
    first = jnp.where(seq == 0, mine, came)
    second = jnp.where(seq == 0, came, mine)
    inputs_low = jnp.concatenate([first, second], axis=1).reshape(count_tok, width)
    grad_came = wires.swap(out_grad)
    ga = Gather(wires, [regroup(qkv_weight), small_cols])
    gc = Gather(wires, [out_weight, fc1_weight])
    gd = Gather(wires, [fc2_weight])
    ga.step()
    gc.step(ga.flight)
    ga.step()
    gd.step(gc.flight)
    gc.step(ga.sends)
    ga.step(gc.sends)
    qkv_full, small_all = ga.result()
    small_full = small_all.T[:n_small].astype(F32)
    norm1_gain, norm1_shift, q_shift, v_shift, out_shift, norm2_gain, norm2_shift, fc2_shift = [
        small_full[i] for i in range(8)
    ]
    fc1_shift = small_full[8:n_small].reshape(wide, devices, m).transpose(1, 0, 2).reshape(ff)
    inputs_low = gate(inputs_low, grad_came)
    seg = own_rows(segments)
    seg_flat = seg.reshape(count_tok)
    mask = (seg_flat >= 0).astype(F32)

    inputs = inputs_low.astype(F32)
    normed1, inverse1 = norm_stats(inputs)
    attn_in = (normed1 * norm1_gain + norm1_shift).astype(BF)
    attn_in = gate(attn_in, gd.flight)
    qkv_out = dot_plain(attn_in, qkv_full)
    pairs = width // (4 * HEAD_DIM)
    joined_shift = jnp.stack([q_shift, jnp.zeros_like(q_shift), v_shift])
    joined_shift = joined_shift.reshape(3, 2 * pairs, 2 * HEAD_DIM).transpose(1, 0, 2).reshape(3 * width)
    joined = (qkv_out + joined_shift).astype(BF)
    mixed, logs = attend(joined, seg, 0, 2 * pairs)
    gc.step((mixed,))
    gd.step(gc.sends)
    out_full, fc1_full = gc.result()
    mixed = gate(mixed, gd.sends)
    resid1 = inputs + dot_plain(mixed, out_full) + out_shift
    normed2, inverse2 = norm_stats(resid1)
    mlp_in = (normed2 * norm2_gain + norm2_shift).astype(BF)
    activated_low, slope, act_stay, act_go = widen(wires, mlp_in, fc1_full, fc1_shift)
    gd.step((slope,))
    (fc2_full,) = gd.result()
    resid2 = resid1 + dot_plain(activated_low, fc2_full) + fc2_shift

    learn_scale = learn_gain.astype(F32)
    normed3, inverse3 = norm_stats(resid2)
    normed3_out = normed3 * learn_scale + learn_bias.astype(F32)
    map_weight = maps_weight.astype(F32)
    logits = dot_second(normed3_out, map_weight, HIGH) + maps_bias.astype(F32)
    sigmas = jax.nn.sigmoid(logits)
    map_vals = sigmas * mask[:, None]
    row_index = jnp.arange(count_tok, dtype=jnp.int32) // row_len
    owner = jnp.where(seg_flat >= 0, row_index * IMG_ROW + seg_flat, -1)
    select = (owner[:, None] == jnp.arange(records, dtype=jnp.int32)[None, :]).astype(F32)
    token_weights = (select[:, :, None] * map_vals[:, None, :]).reshape(count_tok, records * NTOK)
    sums = dot_first(token_weights, resid2, HIGH)
    counts = jnp.sum(select * mask[:, None], axis=0)
    divisor = jnp.maximum(counts, 1.0)
    positions = own_rows(dest_shard * capacity + dest_slot).reshape(records)
    routing = (
        (positions[None, :] == jnp.arange(2 * capacity, dtype=jnp.int32)[:, None])
        & (counts > 0.0)[None, :]
    ).astype(BF)
    pooled_here = (sums.reshape(records, NTOK * width) / divisor[:, None]).astype(BF)
    pooled_all = dot_plain(routing, pooled_here).astype(BF).reshape(2, capacity, NTOK * width)
    pooled_came = wires.swap(pick(pooled_all, 1 - seq, 0))
    pooled = (pick(pooled_all, seq, 0).astype(F32) + pooled_came.astype(F32)).astype(BF)
    pooled = pooled.reshape(1, capacity, NTOK, width)

    grad_own = out_grad.reshape(capacity, NTOK * width)
    grad_far = grad_came.reshape(capacity, NTOK * width)
    grad_pos = jnp.where(
        seq == 0,
        jnp.concatenate([grad_own, grad_far], axis=0),
        jnp.concatenate([grad_far, grad_own], axis=0),
    )
    grad_records = (dot_first(routing, grad_pos) / divisor[:, None]).astype(BF)
    grad_records = grad_records.reshape(records * NTOK, width).astype(F32)

    grad_resid2 = dot_plain(token_weights, grad_records, HIGH)
    grad_maps_all = dot_second(resid2, grad_records, HIGH).reshape(count_tok, records, NTOK)
    grad_map_vals = jnp.sum(grad_maps_all * select[:, :, None], axis=1)
    grad_logits = grad_map_vals * mask[:, None] * sigmas * (1.0 - sigmas)
    grad_maps_weight = dot_first(grad_logits, normed3_out, HIGH)
    grad_maps_bias = jnp.sum(grad_logits, axis=0)
    grad_normed3 = dot_plain(grad_logits, map_weight, HIGH)
    back_three, grad_learn_gain, grad_learn_bias = norm_backward(
        grad_normed3, normed3, inverse3, learn_scale
    )
    grad_resid2 = grad_resid2 + back_three
    grad_branch2 = grad_resid2.astype(BF)
    s_fc2 = Scatter(wires)
    grad_branch2 = gate(grad_branch2, s_fc2.add(activated_low, act_stay, act_go, grad_branch2))
    grad_fc2_shift = jnp.sum(grad_branch2.astype(F32), axis=0)
    grad_activ = dot_second(grad_branch2, fc2_full).astype(BF)
    grad_hidden = (grad_activ.astype(F32) * slope.astype(F32)).astype(BF)
    grad_hidden = gate(grad_hidden, (s_fc2.inner(), pooled, grad_fc2_shift, grad_maps_weight))
    s_fc1 = Scatter(wires)
    grad_hidden = gate(grad_hidden, s_fc1.add(mlp_in, *halves(wires, mlp_in), grad_hidden)[:1])
    grad_fc1_shift = jnp.sum(grad_hidden.astype(F32), axis=0)
    grad_hidden = gate(grad_hidden, s_fc2.relay())
    grad_normed2 = dot_second(grad_hidden, fc1_full)
    back_two, grad_norm2_gain, grad_norm2_shift = norm_backward(
        grad_normed2, normed2, inverse2, norm2_gain
    )
    grad_resid1 = grad_resid2 + back_two
    grad_branch1 = grad_resid1.astype(BF)
    grad_branch1 = gate(grad_branch1, (s_fc1.inner(), grad_fc1_shift))
    s_a = Scatter(wires)
    sent = s_a.add(mixed, *halves(wires, mixed), grad_branch1)
    grad_out_shift = jnp.sum(grad_branch1.astype(F32), axis=0)
    grad_branch1 = gate(grad_branch1, sent)
    grad_mixed = dot_second(grad_branch1, out_full).astype(BF)
    grad_mixed = gate(grad_mixed, (s_fc2.terms, grad_out_shift, s_fc1.relay()))
    grad_a = attend_back(joined, logs[:, :pairs], grad_mixed, seg, 0, pairs)
    attn_stay, attn_go = halves(wires, attn_in)
    sent = s_a.add(attn_in, attn_stay, attn_go, grad_a)
    grad_mixed = gate(grad_mixed, (sent, s_fc1.terms))
    grad_b = attend_back(joined, logs[:, pairs:], grad_mixed, seg, pairs, pairs)
    z_one = Outer(wires, [s_fc2, s_fc1], (grad_b,))
    grad_b = gate(grad_b, (s_a.inner(), z_one.sends))
    s_b = Scatter(wires)
    sent = s_b.add(attn_in, attn_stay, attn_go, grad_b)
    grad_a, grad_b = gate((grad_a, grad_b), sent)
    part = 6 * pairs * HEAD_DIM
    grad_a = gate(grad_a, s_a.relay())
    grad_normed1 = dot_second(grad_a, qkv_full[:, :part])
    grad_b = gate(grad_b, (s_b.inner(), grad_normed1, z_one.terms))
    grad_normed1 = grad_normed1 + dot_second(grad_b, qkv_full[:, part:])
    grad_normed1 = gate(grad_normed1, (s_a.terms, s_b.relay()))
    back_one, grad_norm1_gain, grad_norm1_shift = norm_backward(
        grad_normed1, normed1, inverse1, norm1_gain
    )
    sums_here = jnp.concatenate([jnp.sum(g.astype(F32), axis=0) for g in (grad_a, grad_b)])
    sums_here = sums_here.reshape(2 * pairs, 3, 2 * HEAD_DIM)
    sum_q, sum_v = sums_here[:, 0].reshape(width), sums_here[:, 2].reshape(width)
    little = jnp.concatenate(
        [
            jnp.stack(
                [
                    grad_norm1_gain,
                    grad_norm1_shift,
                    sum_q,
                    sum_v,
                    grad_out_shift,
                    grad_norm2_gain,
                    grad_norm2_shift,
                    grad_fc2_shift,
                    grad_learn_gain,
                    grad_learn_bias,
                    jnp.pad(grad_maps_bias, (0, width - NTOK)),
                ]
            ),
            grad_maps_weight,
            grad_fc1_shift.reshape(wide, width),
        ],
        axis=0,
    )
    z_two = Outer(wires, [s_a, s_b])
    little = jnp.pad(little, ((0, -little.shape[0] % 8), (0, 0)))
    little = sum_everywhere(wires, gate(little, z_two.sends), z_two.terms)
    grad_rows = (grad_resid1 + back_one).reshape(rows_here, row_len, width)
    grad_away = lax.dynamic_slice_in_dim(grad_rows, (1 - seq) * slots_half, slots_half, 1)
    grad_back = wires.swap(grad_away)
    grad_kept = lax.dynamic_slice_in_dim(grad_rows, seq * slots_half, slots_half, 1)
    grad_held = jnp.where(
        seq == 0,
        jnp.concatenate([grad_kept, grad_back], axis=0),
        jnp.concatenate([grad_back, grad_kept], axis=0),
    )
    z_two.terms = gate(z_two.terms, grad_held)
    lane = 2 * HEAD_DIM

    def same(column):
        return column

    def spread(first):
        return lambda column: (
            column // lane % 3 * width + (first + column // (3 * lane)) * lane + column % lane
        )

    z_one.terms = gate(z_one.terms, z_two.sends)
    done_fc2, done_fc1 = z_one.result(
        [(wide * m, width), (m, ff)], [(0, same), (1, same)]
    )
    done_two = z_two.result(
        [(m, width), (m, 3 * width)], [(0, same), (1, spread(0)), (1, spread(pairs))]
    )
    done_out, done_qkv = done_two[0], done_two[1]
    if z_two.plain:
        done_qkv = jnp.concatenate(done_two[1:], axis=1).reshape(m, 2 * pairs, 3, lane)
        done_qkv = done_qkv.transpose(0, 2, 1, 3).reshape(m, 3 * width)
    place = lax.axis_index("rows") * 2 + seq
    held = lax.dynamic_slice_in_dim(little[:8], place * m, m, 1)
    held_fc1 = lax.dynamic_slice_in_dim(
        little[11 + NTOK : 11 + NTOK + wide].reshape(ff), place * wide * m, wide * m, 0
    )
    return (
        pooled,
        grad_held,
        held[0],
        held[1],
        done_qkv,
        held[2:4],
        done_out,
        held[4],
        held[5],
        held[6],
        done_fc1,
        held_fc1,
        done_fc2,
        held[7],
        little[8],
        little[9],
        little[11 : 11 + NTOK],
        little[10, :NTOK],
    )


def solution(mesh):
    both = ("rows", "seq")
    in_specs = (
        P("rows", "seq", None),
        P("rows", None),
        P("rows", "seq"),
        P("rows", None),
        P("rows", None),
        P(both),
        P(both),
        P(both, None),
        P(None, both),
        P(both, None),
        P(both),
        P(both),
        P(both),
        P(both, None),
        P(both),
        P(both, None),
        P(both),
        P(),
        P(),
        P(),
        P(),
        P("rows", "seq", None, None),
    )
    out_specs = (
        P("rows", "seq", None, None),
        P("rows", "seq", None),
        P(both),
        P(both),
        P(both, None),
        P(None, both),
        P(both, None),
        P(both),
        P(both),
        P(both),
        P(both, None),
        P(both),
        P(both, None),
        P(both),
        P(),
        P(),
        P(),
        P(),
    )
    return jax.shard_map(shards, mesh=mesh, in_specs=in_specs, out_specs=out_specs, check_vma=False)
```
